512 devices in a mesh: blk: 32 (over x_lo, y, core), tm: 16 (over z, x_hi).
Axes of the slice: x: 4 (x_hi: 2, x_lo: 2; x = x_hi * 2 + x_lo), y: 8, z: 8, core: 2. Of those that a mesh axis runs over, the one named last changes fastest.
Arguments:
- clips: bfloat16 [32, 32, 16, 36, 256], P('blk', 'tm'), may hold values from -6 to 6
- cotangent: bfloat16 [32, 32, 16, 36, 256], P('blk', 'tm'), may hold values from -6 to 6
- conv_master: float32 [3072, 256], P('blk'), may hold values from -0.125 to 0.125
- first_moment: float32 [3072, 256], P('blk'), may hold values from -3 to 3
- second_moment: float32 [3072, 256], P('blk'), may hold values from 0.1 to 100
- norm_gain: float32 [256], replicated, may hold values from 0.5 to 1.5
- norm_bias: float32 [256], replicated, may hold values from -3 to 3
Outputs:
- block_out: bfloat16 [32, 32, 16, 36, 256], P('blk', 'tm')
- input_grad: bfloat16 [32, 32, 16, 36, 256], P('blk', 'tm')
- new_master: float32 [3072, 256], P('blk')
- new_first: float32 [3072, 256], P('blk')
- new_second: float32 [3072, 256], P('blk')
- norm_grads: float32 [2, 256], replicated
The draws below stay inside these ranges and needn't reach their ends.
All inputs are finite; a program needn't handle non-finite values.
Results may differ from the reference program's by a relative error of at most 0.0063.
Values may be sent and summed in bfloat16 or wider, within the bound.
A program may use at most 64 MiB of HBM per device.

```python
import math
import jax
import jax.numpy as jnp
from jax import lax

C = 256
H = 16
W = 36
GROUPS = 32
CLIPS = 32
FRAMES = 32


def block_scale(rng, shape, pieces, low, high):
    def one(position, blocks):
        draws = jax.random.uniform(jax.random.fold_in(jax.random.fold_in(rng, 6), position), (blocks,), jnp.float32, low / len(pieces), high / len(pieces))
        return jnp.repeat(jnp.exp(draws), shape[position] // blocks).reshape((-1,) + (1,) * (len(shape) - position - 1))

    factor_of = one(*pieces[0])
    for cut in pieces[1:]:
        factor_of = factor_of * one(*cut)
    return factor_of


def normal_values(rng, shape, deviation, bound, pieces=(), dtype=jnp.bfloat16):
    loudness = block_scale(rng, shape, pieces, -0.22, 0.18) if pieces else 1.0
    array = jax.random.normal(rng, shape, jnp.float32) * deviation * loudness
    return jnp.minimum(jnp.maximum(array, -bound), bound).astype(dtype)


def setup_inputs(seed: int = 0) -> dict:
    arg_keys = jax.random.split(jax.random.key(seed), 8)
    clips = normal_values(arg_keys[0], (CLIPS, FRAMES, H, W, C), 1.0, 6.0, ((0, 32), (1, 16)))
    cotangent = normal_values(arg_keys[1], (CLIPS, FRAMES, H, W, C), 1.0, 6.0, ((0, 32), (1, 16)))
    conv_master = normal_values(arg_keys[2], (12 * C, C), (9 * C) ** -0.5, 0.125, ((0, 32),), jnp.float32)
    first_moment = normal_values(arg_keys[3], (12 * C, C), 0.5, 3.0, ((0, 32),), jnp.float32)
    second_moment = jnp.clip(jnp.exp(math.log(100.0) - 6.9077553 * jax.random.uniform(arg_keys[4], (12 * C, C), jnp.float32) ** block_scale(arg_keys[4], (12 * C, C), ((0, 32),), -0.2, 0.2)), 0.1, 100.0)
    norm_gain = jnp.clip(jax.random.uniform(arg_keys[5], (C,), jnp.float32, 0.5, 1.5), 0.5, 1.5)
    norm_bias = normal_values(arg_keys[6], (C,), 0.5, 3.0, (), jnp.float32)
    return dict(clips=clips, cotangent=cotangent, conv_master=conv_master, first_moment=first_moment, second_moment=second_moment, norm_gain=norm_gain, norm_bias=norm_bias)


beta_one = 0.9
beta_two = 0.999
learn_rate = 0.003
adam_eps = 1e-08
bias_first = 1.0 - 0.9 ** 10
bias_second = 1.0 - 0.999 ** 10

def norm_act(field, gain, bias):
    shape = field.shape
    grouped = field.reshape(shape[:-3] + (shape[-3] * shape[-2], GROUPS, shape[-1] // GROUPS))
    center = lax.optimization_barrier(jnp.mean(grouped, axis=(-3, -1), keepdims=True))
    spread = lax.optimization_barrier(jnp.mean((grouped - center) ** 2, axis=(-3, -1), keepdims=True))
    normed = ((grouped - center) * lax.rsqrt(spread + 1e-05)).reshape(shape)
    return jax.nn.silu(normed * gain + bias)

def clip_pass(clip, grad_out, weights, gain, bias):
    frames, height, width, channels = clip.shape
    f32 = jnp.float32
    inputs32 = clip.astype(f32)
    act32, pullback = jax.vjp(norm_act, inputs32, gain, bias)
    act = act32.astype(jnp.bfloat16)
    act_padded = jnp.pad(act, ((0, 0), (1, 1), (1, 1), (0, 0)))
    space32 = jnp.zeros((frames, height, width, channels), f32)
    for row_tap in range(3):
        for col_tap in range(3):
            tap_index = 3 * row_tap + col_tap
            window = act_padded[:, row_tap:row_tap + height, col_tap:col_tap + width, :]
            tap = weights[tap_index * channels:(tap_index + 1) * channels]
            space32 = space32 + jnp.einsum('fhwc,cd->fhwd', window.astype(f32), tap.astype(f32))
    space = space32.astype(jnp.bfloat16)
    space_padded = jnp.pad(space, ((1, 1), (0, 0), (0, 0), (0, 0)))
    grad_padded = jnp.pad(grad_out, ((1, 1), (0, 0), (0, 0), (0, 0)))
    temporal = jnp.zeros((frames, height, width, channels), f32)
    space_grad32 = jnp.zeros((frames, height, width, channels), f32)
    temporal_grads = []
    for frame_tap in range(3):
        tap = weights[(9 + frame_tap) * channels:(10 + frame_tap) * channels].astype(f32)
        temporal = temporal + jnp.einsum('fhwc,cd->fhwd', space_padded[frame_tap:frame_tap + frames].astype(f32), tap)
        space_grad32 = space_grad32 + jnp.einsum('fhwd,cd->fhwc', grad_padded[2 - frame_tap:2 - frame_tap + frames].astype(f32), tap)
        temporal_grads.append(jnp.einsum('fhwc,fhwd->cd', space_padded[frame_tap:frame_tap + frames].astype(f32), grad_out.astype(f32)))
    block_out = (inputs32 + temporal).astype(jnp.bfloat16)
    space_grad = space_grad32.astype(jnp.bfloat16)
    sgrad_padded = jnp.pad(space_grad, ((0, 0), (1, 1), (1, 1), (0, 0)))
    act_grad = jnp.zeros((frames, height, width, channels), f32)
    spatial_grads = []
    for row_tap in range(3):
        for col_tap in range(3):
            tap_index = 3 * row_tap + col_tap
            tap = weights[tap_index * channels:(tap_index + 1) * channels].astype(f32)
            window = act_padded[:, row_tap:row_tap + height, col_tap:col_tap + width, :]
            spatial_grads.append(jnp.einsum('fhwc,fhwd->cd', window.astype(f32), space_grad.astype(f32)))
            back_window = sgrad_padded[:, 2 - row_tap:2 - row_tap + height, 2 - col_tap:2 - col_tap + width, :]
            act_grad = act_grad + jnp.einsum('fhwd,cd->fhwc', back_window.astype(f32), tap)
    input_term, gain_grad, bias_grad = pullback(act_grad)
    input_grad = (grad_out.astype(f32) + input_term).astype(jnp.bfloat16)
    gradient = jnp.concatenate(spatial_grads + temporal_grads, axis=0)
    return (block_out, input_grad, gradient, jnp.stack([gain_grad, bias_grad]))

def reference(clips, cotangent, conv_master, first_moment, second_moment, norm_gain, norm_bias):
    weights = conv_master.astype(jnp.bfloat16)

    def clip_step(carry, pair):
        block_out, input_grad, gradient, norm_part = clip_pass(pair[0], pair[1], weights, norm_gain, norm_bias)
        return ((carry[0] + gradient, carry[1] + norm_part), (block_out, input_grad))
    start_carry = (jnp.zeros(conv_master.shape, jnp.float32), jnp.zeros((2, conv_master.shape[1]), jnp.float32))
    (gradient, norm_grads), (block_out, input_grad) = lax.scan(clip_step, start_carry, (clips, cotangent))
    new_first = beta_one * first_moment + (1.0 - beta_one) * gradient
    new_second = beta_two * second_moment + (1.0 - beta_two) * gradient * gradient
    update = new_first / bias_first / (jnp.sqrt(new_second / bias_second) + adam_eps)
    new_master = conv_master - learn_rate * update
    return (block_out, input_grad, new_master, new_first, new_second, norm_grads)
```

```python
import jax
import jax.numpy as jnp
from jax import lax
from jax.experimental import pallas as pl
from jax.experimental.pallas import tpu as pltpu
from jax.sharding import PartitionSpec as P

GROUPS = 32


beta_one = 0.9
beta_two = 0.999
learn_rate = 0.003
adam_eps = 1e-08
bias_first = 1.0 - 0.9**10
bias_second = 1.0 - 0.999**10


def extended(block, sides, width):
    for axis, dim in sides:
        count = lax.axis_size(axis)
        forward = [(i, i + 1) for i in range(count - 1)]
        backward = [(target, source) for source, target in forward]
        low = lax.ppermute(
            lax.slice_in_dim(block, block.shape[dim] - width, None, axis=dim), axis, forward
        )
        high = lax.ppermute(lax.slice_in_dim(block, 0, width, axis=dim), axis, backward)
        block = jnp.concatenate([low, block, high], axis=dim)
    return block


def norm_act(field, gain, bias):
    shape = field.shape
    grouped = field.reshape(shape[:-3] + (shape[-3] * shape[-2], GROUPS, shape[-1] // GROUPS))
    center = jnp.mean(grouped, axis=(-3, -1), keepdims=True)
    spread = jnp.mean((grouped - center) ** 2, axis=(-3, -1), keepdims=True)
    normed = ((grouped - center) * lax.rsqrt(spread + 1e-05)).reshape(shape)
    return jax.nn.silu(normed * gain + bias)


def adam_update(gradient, master, first, second):
    new_first = beta_one * first + (1.0 - beta_one) * gradient
    new_second = beta_two * second + (1.0 - beta_two) * gradient * gradient
    update = new_first / bias_first / (jnp.sqrt(new_second / bias_second) + adam_eps)
    return (master - learn_rate * update, new_first, new_second)

MESH = pl.DeviceIdType.MESH
VMEM = pl.BlockSpec(memory_space=pltpu.VMEM)


def place():
    me = lax.axis_index("blk")
    return me // 16, lax.rem(me // 2, 8), lax.rem(me, 2), lax.axis_index("tm")


def owner(x, y, c):
    return x * 16 + lax.rem(y + 8, 8) * 2 + c


def greet(peers):
    barrier = pltpu.get_barrier_semaphore()
    for peer in peers:
        pl.semaphore_signal(barrier, inc=1, device_id=peer, device_id_type=MESH)
    pl.semaphore_wait(barrier, len(peers))


def send(src, dst, send_sem, recv_sem, peer):
    copy = pltpu.make_async_remote_copy(
        src_ref=src,
        dst_ref=dst,
        send_sem=send_sem,
        recv_sem=recv_sem,
        device_id=peer,
        device_id_type=MESH,
    )
    copy.start()
    return copy


def gather_kernel(w_ref, out_ref, ring_send, ring_recv, pair_send, pair_recv, x_send, x_recv):
    x, y, c, t = place()
    partner = (owner(x, y, 1 - c), t)
    across = (owner(1 - x, y, c), t)
    ring = ((owner(x, y + 1, c), t), (owner(x, y - 1, c), t))
    greet([partner, across, ring[0], ring[1]])
    started = []

    def pass_on(src, k, offset):
        slot = k * 8 + offset % 8
        dst = out_ref.at[owner(x if k == 0 else 1 - x, y + offset, c)]
        started.append(send(src, dst, pair_send.at[slot], pair_recv.at[slot], partner))

    def hop(src, d, s, k):
        offset = -s if d == 0 else s
        dst = out_ref.at[owner(x if k == 0 else 1 - x, y + offset, c)]
        copy = send(src, dst, ring_send.at[d, s, k], ring_recv.at[d, s, k], ring[d])
        started.append(copy)
        return copy

    mine = owner(x, y, c)
    x_copy = send(w_ref, out_ref.at[mine], x_send, x_recv, across)
    copies = {}
    for d in range(2):
        copies[d, 0] = hop(w_ref, d, 0, 0)
    pass_on(w_ref, 0, 0)
    out_ref[mine] = w_ref[...]
    x_copy.wait_recv()
    other = out_ref.at[owner(1 - x, y, c)]
    for d in range(2):
        copies[d, 1] = hop(other, d, 0, 1)
    pass_on(other, 1, 0)
    for s in range(1, 5):
        for k in range(2):
            for d in range(2):
                if s == 4 and k != d:
                    continue
                offset = -s if d == 0 else s
                copies[d, k].wait_recv()
                block = out_ref.at[owner(x if k == 0 else 1 - x, y + offset, c)]
                if s < 3 or (s == 3 and k == d):
                    copies[d, k] = hop(block, d, s, k)
                pass_on(block, k, offset)
    x_copy.wait_send()
    for copy in started:
        copy.wait_send()
    for slot in range(16):
        k, offset = slot // 8, slot % 8
        block = out_ref.at[owner(x if k == 0 else 1 - x, y + offset, 1 - c)]
        pltpu.make_async_remote_copy(
            src_ref=w_ref,
            dst_ref=block,
            send_sem=pair_send.at[slot],
            recv_sem=pair_recv.at[slot],
            device_id=partner,
            device_id_type=MESH,
        ).wait_recv()


def gather_weights(rows):
    dma = pltpu.SemaphoreType.DMA
    return pl.pallas_call(
        gather_kernel,
        out_shape=jax.ShapeDtypeStruct((32,) + rows.shape, rows.dtype),
        in_specs=[VMEM],
        out_specs=VMEM,
        scratch_shapes=[dma((2, 4, 2)), dma((2, 4, 2)), dma((16,)), dma((16,)), dma(()), dma(())],
        compiler_params=pltpu.CompilerParams(collective_id=0, has_side_effects=True),
        name="gather_weights",
    )(rows)


PAIR_ORDER = (4, 3, -3, 2, -2, 1, -1, 0)


def reduce_kernel(
    g_ref,
    n_ref,
    out_ref,
    norm_ref,
    pair_buf,
    ring_src,
    ring_dst,
    x_src,
    x_dst,
    held,
    z_dst,
    h_src,
    h_dst,
    z_src,
    n_pair,
    n_y_src,
    n_y,
    n_x_src,
    n_x,
    n_z_src,
    n_z,
    n_h_src,
    n_h,
    pair_s,
    pair_r,
    ring_s,
    ring_r,
    zs_s,
    zs_r,
    zg_s,
    zg_r,
    one_s,
    one_r,
    ny_s,
    ny_r,
    nz_s,
    nz_r,
):
    f32 = jnp.float32
    x, y, c, t = place()
    z, h = t // 2, lax.rem(t, 2)
    mine = owner(x, y, c)
    partner = (owner(x, y, 1 - c), t)
    across = (owner(1 - x, y, c), t)
    far = (mine, z * 2 + 1 - h)
    y_peers = [(owner(x, y + i, c), t) for i in range(1, 8)]
    z_peers = [(mine, lax.rem(z + i, 8) * 2 + h) for i in range(1, 8)]
    ring = (y_peers[0], y_peers[6])
    greet([partner, across, far] + y_peers + z_peers)
    started = []

    def go(*args):
        copy = send(*args)
        started.append(copy)
        return copy

    norm_pair = go(n_ref, n_pair, one_s.at[0], one_r.at[0], partner)
    pair = []
    for m, offset in enumerate(PAIR_ORDER):
        target = lax.rem(y + offset + 8, 8)
        pair.append(
            go(g_ref.at[:, target, 1 - c], pair_buf.at[m], pair_s.at[m], pair_r.at[m], partner)
        )
    arrived = {}
    waited = set()

    def local(offset, k):
        m = PAIR_ORDER.index(offset)
        if m not in waited:
            pair[m].wait_recv()
            waited.add(m)
        return g_ref[k, lax.rem(y + offset + 8, 8), c] + pair_buf[m, k]

    for s in range(4):
        for k in range(2):
            for d in range(2):
                if s == 0 and k != d:
                    continue
                offset = 4 if s == 0 else (4 - s if d == 0 else s - 4)
                value = local(offset, k)
                if (d, k) in arrived:
                    arrived[d, k].wait_recv()
                    value = value + ring_dst[d, s - 1, k].astype(f32)
                ring_src[d, s, k] = value.astype(ring_src.dtype)
                arrived[d, k] = go(
                    ring_src.at[d, s, k],
                    ring_dst.at[d, s, k],
                    ring_s.at[d, s, k],
                    ring_r.at[d, s, k],
                    ring[d],
                )
        if s == 0:
            norm_pair.wait_recv()
            part = n_ref[...] + n_pair[...]
            n_y_src[...] = part
            n_y[y] = part
            norm_y = [
                go(n_y_src, n_y.at[y], ny_s.at[i], ny_r.at[i], peer)
                for i, peer in enumerate(y_peers)
            ]
        if s == 1:
            for copy in norm_y:
                copy.wait_recv()
            part = n_y[0]
            for i in range(1, 8):
                part = part + n_y[i]
            n_x_src[...] = part
            norm_x = go(n_x_src, n_x, one_s.at[1], one_r.at[1], across)
        if s == 2:
            norm_x.wait_recv()
            part = n_x_src[...] + n_x[...]
            n_z_src[...] = part
            n_z[z] = part
            norm_z = [
                go(n_z_src, n_z.at[z], nz_s.at[i], nz_r.at[i], peer)
                for i, peer in enumerate(z_peers)
            ]
        if s == 3:
            for copy in norm_z:
                copy.wait_recv()
            part = n_z[0]
            for i in range(1, 8):
                part = part + n_z[i]
            n_h_src[...] = part
            norm_h = go(n_h_src, n_h, one_s.at[2], one_r.at[2], far)

    totals = []
    for k in range(2):
        value = local(0, k)
        for d in range(2):
            arrived[d, k].wait_recv()
            value = value + ring_dst[d, 3, k].astype(f32)
        totals.append(value)
    keep = jnp.where(x == 0, totals[0], totals[1])
    x_src[...] = jnp.where(x == 0, totals[1], totals[0])
    x_copy = go(x_src, x_dst, one_s.at[3], one_r.at[3], across)
    x_copy.wait_recv()
    value = keep + x_dst[...]
    for p in range(8):
        held[p] = value[(p // 2) * 24 : (p // 2) * 24 + 24, (p % 2) * 128 : (p % 2) * 128 + 128]
    scatter = [
        go(held.at[lax.rem(z + i + 1, 8)], z_dst.at[z], zs_s.at[i], zs_r.at[i], peer)
        for i, peer in enumerate(z_peers)
    ]
    z_dst[z] = held[z]
    for copy in scatter:
        copy.wait_recv()
    part = z_dst[0]
    for i in range(1, 8):
        part = part + z_dst[i]
    h_src[...] = part
    h_copy = go(h_src, h_dst, one_s.at[4], one_r.at[4], far)
    norm_h.wait_recv()
    norm_ref[...] = n_h_src[...] + n_h[...]
    h_copy.wait_recv()
    part = h_src[...] + h_dst[...]
    z_src[...] = part
    out_ref[z] = part
    spread = [
        go(z_src, out_ref.at[z], zg_s.at[i], zg_r.at[i], peer) for i, peer in enumerate(z_peers)
    ]
    for copy in spread:
        copy.wait_recv()
    for copy in started:
        copy.wait_send()


def reduce_gradient(gradient, norms):
    f32, bf16 = jnp.float32, jnp.bfloat16
    dma, vmem = pltpu.SemaphoreType.DMA, pltpu.VMEM
    small = vmem((8, 128), f32)
    eight = vmem((8, 8, 128), f32)
    return pl.pallas_call(
        reduce_kernel,
        out_shape=(
            jax.ShapeDtypeStruct((8, 24, 128), f32),
            jax.ShapeDtypeStruct((8, 128), f32),
        ),
        in_specs=[VMEM, VMEM],
        out_specs=(VMEM, VMEM),
        scratch_shapes=[
            vmem((8, 2, 96, 256), f32),
            vmem((2, 4, 2, 96, 256), bf16),
            vmem((2, 4, 2, 96, 256), bf16),
            vmem((96, 256), f32),
            vmem((96, 256), f32),
            vmem((8, 24, 128), f32),
            vmem((8, 24, 128), f32),
            vmem((24, 128), f32),
            vmem((24, 128), f32),
            vmem((24, 128), f32),
            small,
            small,
            eight,
            small,
            small,
            small,
            eight,
            small,
            small,
            dma((8,)),
            dma((8,)),
            dma((2, 4, 2)),
            dma((2, 4, 2)),
            dma((7,)),
            dma((7,)),
            dma((7,)),
            dma((7,)),
            dma((5,)),
            dma((5,)),
            dma((7,)),
            dma((7,)),
            dma((7,)),
            dma((7,)),
        ],
        compiler_params=pltpu.CompilerParams(
            collective_id=1, has_side_effects=True, vmem_limit_bytes=40 * 2**20
        ),
        name="reduce_gradient",
    )(gradient.reshape(2, 8, 2, 96, 256), norms)


def shards(clips, cotangent, conv_master, first_moment, second_moment, norm_gain, norm_bias):
    f32 = jnp.float32
    frames, height, width, channels = (
        clips.shape[1],
        clips.shape[2],
        clips.shape[3],
        clips.shape[4],
    )
    weights = gather_weights(conv_master.astype(jnp.bfloat16)).reshape(12 * channels, channels)
    inputs32 = clips.astype(f32)
    act32, pullback = jax.vjp(norm_act, inputs32, norm_gain, norm_bias)
    act = act32.astype(jnp.bfloat16)
    act_padded = jnp.pad(act, ((0, 0), (0, 0), (1, 1), (1, 1), (0, 0)))
    space32 = jnp.zeros(clips.shape, f32)
    for row_tap in range(3):
        for col_tap in range(3):
            tap_index = 3 * row_tap + col_tap
            window = act_padded[:, :, row_tap : row_tap + height, col_tap : col_tap + width, :]
            tap = weights[tap_index * channels : (tap_index + 1) * channels]
            space32 = space32 + jnp.einsum(
                "bfhwc,cd->bfhwd", window, tap, preferred_element_type=f32
            )
    space = space32.astype(jnp.bfloat16)
    space_padded = extended(space, (("tm", 1),), 1)
    temporal = jnp.zeros(clips.shape, f32)
    for frame_tap in range(3):
        tap = weights[(9 + frame_tap) * channels : (10 + frame_tap) * channels]
        temporal = temporal + jnp.einsum(
            "bfhwc,cd->bfhwd",
            space_padded[:, frame_tap : frame_tap + frames],
            tap,
            preferred_element_type=f32,
        )
    block_out = (inputs32 + temporal).astype(jnp.bfloat16)
    back_weights = weights
    grad_padded = extended(cotangent, (("tm", 1),), 1)
    space_grad32 = jnp.zeros(clips.shape, f32)
    temporal_grads = []
    for frame_tap in range(3):
        tap = back_weights[(9 + frame_tap) * channels : (10 + frame_tap) * channels]
        space_grad32 = space_grad32 + jnp.einsum(
            "bfhwd,cd->bfhwc",
            grad_padded[:, 2 - frame_tap : 2 - frame_tap + frames],
            tap,
            preferred_element_type=f32,
        )
        temporal_grads.append(
            jnp.einsum(
                "bfhwc,bfhwd->cd",
                space,
                grad_padded[:, 2 - frame_tap : 2 - frame_tap + frames],
                preferred_element_type=f32,
            )
        )
    space_grad = space_grad32.astype(jnp.bfloat16)
    sgrad_padded = jnp.pad(space_grad, ((0, 0), (0, 0), (1, 1), (1, 1), (0, 0)))
    act_grad = jnp.zeros(clips.shape, f32)
    spatial_grads = []
    for row_tap in range(3):
        for col_tap in range(3):
            tap_index = 3 * row_tap + col_tap
            tap = back_weights[tap_index * channels : (tap_index + 1) * channels]
            window = act_padded[:, :, row_tap : row_tap + height, col_tap : col_tap + width, :]
            spatial_grads.append(
                jnp.einsum("bfhwc,bfhwd->cd", window, space_grad, preferred_element_type=f32)
            )
            back_window = sgrad_padded[
                :, :, 2 - row_tap : 2 - row_tap + height, 2 - col_tap : 2 - col_tap + width, :
            ]
            act_grad = act_grad + jnp.einsum(
                "bfhwd,cd->bfhwc", back_window, tap, preferred_element_type=f32
            )
    input_term, gain_grad, bias_grad = pullback(act_grad)
    input_grad = (cotangent.astype(f32) + input_term).astype(jnp.bfloat16)
    local_gradient = jnp.concatenate(spatial_grads + temporal_grads, axis=0)
    norms = jnp.pad(jnp.concatenate([gain_grad, bias_grad]).reshape(4, 128), ((0, 4), (0, 0)))
    pieces, norm_sums = reduce_gradient(local_gradient, norms)
    norm_grads = norm_sums[:4].reshape(2, channels)
    gradient = pieces.reshape(4, 2, 24, 128).transpose(0, 2, 1, 3).reshape(96, channels)
    new_master, new_first, new_second = adam_update(
        gradient, conv_master, first_moment, second_moment
    )
    return (block_out, input_grad, new_master, new_first, new_second, norm_grads)


def solution(mesh):
    placed = (
        P("blk", "tm", None, None, None),
        P("blk", "tm", None, None, None),
        P("blk", None),
        P("blk", None),
        P("blk", None),
        P(),
        P(),
    )
    return jax.shard_map(
        shards,
        mesh=mesh,
        in_specs=placed,
        out_specs=(
            P("blk", "tm", None, None, None),
            P("blk", "tm", None, None, None),
            P("blk", None),
            P("blk", None),
            P("blk", None),
            P(),
        ),
        check_vma=False,
    )
```

```python
import jax
import jax.numpy as jnp
from jax import lax
from jax.experimental import pallas as pl
from jax.experimental.pallas import tpu as pltpu
from jax.sharding import PartitionSpec as P


beta_one = 0.9
beta_two = 0.999
learn_rate = 0.003
adam_eps = 1e-08
bias_first = 1.0 - 0.9**10
bias_second = 1.0 - 0.999**10


def adam_update(gradient, master, first, second):
    new_first = beta_one * first + (1.0 - beta_one) * gradient
    new_second = beta_two * second + (1.0 - beta_two) * gradient * gradient
    update = new_first / bias_first / (jnp.sqrt(new_second / bias_second) + adam_eps)
    return (master - learn_rate * update, new_first, new_second)

MESH = pl.DeviceIdType.MESH
VMEM = pl.BlockSpec(memory_space=pltpu.VMEM)


def place():
    me = lax.axis_index("blk")
    return me // 16, lax.rem(me // 2, 8), lax.rem(me, 2), lax.axis_index("tm")


def owner(x, y, c):
    return x * 16 + lax.rem(y + 8, 8) * 2 + c


def greet(peers):
    barrier = pltpu.get_barrier_semaphore()
    for peer in peers:
        pl.semaphore_signal(barrier, inc=1, device_id=peer, device_id_type=MESH)
    pl.semaphore_wait(barrier, len(peers))


def send(src, dst, send_sem, recv_sem, peer):
    copy = pltpu.make_async_remote_copy(
        src_ref=src,
        dst_ref=dst,
        send_sem=send_sem,
        recv_sem=recv_sem,
        device_id=peer,
        device_id_type=MESH,
    )
    copy.start()
    return copy


def frame_peers(t):
    me = lax.axis_index("blk")
    return (me, lax.rem(t + 15, 16)), (me, lax.rem(t + 1, 16))


def send_edges(frames, edges, send_sem, recv_sem, low, high):
    return [
        send(frames.at[0], edges.at[1], send_sem.at[1], recv_sem.at[1], low),
        send(frames.at[1], edges.at[0], send_sem.at[0], recv_sem.at[0], high),
    ]


def gather_kernel(
    w_ref,
    cot_ref,
    out_ref,
    edge_ref,
    ring_send,
    ring_recv,
    pair_send,
    pair_recv,
    x_send,
    x_recv,
    edge_send,
    edge_recv,
):
    x, y, c, t = place()
    partner = (owner(x, y, 1 - c), t)
    across = (owner(1 - x, y, c), t)
    ring = ((owner(x, y + 1, c), t), (owner(x, y - 1, c), t))
    low, high = frame_peers(t)
    greet([partner, across, ring[0], ring[1], low, high])
    started = []

    def pass_on(src, k, offset):
        slot = k * 8 + offset % 8
        dst = out_ref.at[owner(x if k == 0 else 1 - x, y + offset, c)]
        started.append(send(src, dst, pair_send.at[slot], pair_recv.at[slot], partner))

    def hop(src, d, s, k):
        offset = -s if d == 0 else s
        dst = out_ref.at[owner(x if k == 0 else 1 - x, y + offset, c)]
        copy = send(src, dst, ring_send.at[d, s, k], ring_recv.at[d, s, k], ring[d])
        started.append(copy)
        return copy

    mine = owner(x, y, c)
    x_copy = send(w_ref, out_ref.at[mine], x_send, x_recv, across)
    copies = {}
    for d in range(2):
        copies[d, 0] = hop(w_ref, d, 0, 0)
    pass_on(w_ref, 0, 0)
    edges = send_edges(cot_ref, edge_ref, edge_send, edge_recv, low, high)
    started.extend(edges)
    out_ref[mine] = w_ref[...]
    x_copy.wait_recv()
    other = out_ref.at[owner(1 - x, y, c)]
    for d in range(2):
        copies[d, 1] = hop(other, d, 0, 1)
    pass_on(other, 1, 0)
    for s in range(1, 5):
        for k in range(2):
            for d in range(2):
                if s == 4 and k != d:
                    continue
                offset = -s if d == 0 else s
                copies[d, k].wait_recv()
                block = out_ref.at[owner(x if k == 0 else 1 - x, y + offset, c)]
                if s < 3 or (s == 3 and k == d):
                    copies[d, k] = hop(block, d, s, k)
                pass_on(block, k, offset)
    x_copy.wait_send()
    for copy in started:
        copy.wait_send()
    for slot in range(16):
        k, offset = slot // 8, slot % 8
        block = out_ref.at[owner(x if k == 0 else 1 - x, y + offset, 1 - c)]
        pltpu.make_async_remote_copy(
            src_ref=w_ref,
            dst_ref=block,
            send_sem=pair_send.at[slot],
            recv_sem=pair_recv.at[slot],
            device_id=partner,
            device_id_type=MESH,
        ).wait_recv()
    for copy in edges:
        copy.wait_recv()


def gather_weights(rows, cotangent):
    dma = pltpu.SemaphoreType.DMA
    return pl.pallas_call(
        gather_kernel,
        out_shape=(
            jax.ShapeDtypeStruct((32,) + rows.shape, rows.dtype),
            jax.ShapeDtypeStruct(cotangent.shape, cotangent.dtype),
        ),
        in_specs=[VMEM, VMEM],
        out_specs=(VMEM, VMEM),
        scratch_shapes=[
            dma((2, 4, 2)),
            dma((2, 4, 2)),
            dma((16,)),
            dma((16,)),
            dma(()),
            dma(()),
            dma((2,)),
            dma((2,)),
        ],
        compiler_params=pltpu.CompilerParams(collective_id=0, has_side_effects=True),
        name="gather_weights",
    )(rows, cotangent)


PAIR_ORDER = (4, 3, -3, 2, -2, 1, -1, 0)


def reduce_kernel(
    g_ref,
    n_ref,
    space_ref,
    out_ref,
    norm_ref,
    edge_ref,
    pair_buf,
    ring_src,
    ring_dst,
    x_src,
    x_dst,
    held,
    z_dst,
    h_src,
    h_dst,
    z_src,
    n_pair,
    n_y_src,
    n_y,
    n_x_src,
    n_x,
    n_z_src,
    n_z,
    n_h_src,
    n_h,
    pair_s,
    pair_r,
    ring_s,
    ring_r,
    zs_s,
    zs_r,
    zg_s,
    zg_r,
    one_s,
    one_r,
    ny_s,
    ny_r,
    nz_s,
    nz_r,
    edge_s,
    edge_r,
):
    f32 = jnp.float32
    x, y, c, t = place()
    z, h = t // 2, lax.rem(t, 2)
    mine = owner(x, y, c)
    partner = (owner(x, y, 1 - c), t)
    across = (owner(1 - x, y, c), t)
    far = (mine, z * 2 + 1 - h)
    y_peers = [(owner(x, y + i, c), t) for i in range(1, 8)]
    z_peers = [(mine, lax.rem(z + i, 8) * 2 + h) for i in range(1, 8)]
    ring = (y_peers[0], y_peers[6])
    low, high = frame_peers(t)
    greet([partner, across, far, low, high] + y_peers + z_peers)
    started = []

    def go(*args):
        copy = send(*args)
        started.append(copy)
        return copy

    norm_pair = go(n_ref, n_pair, one_s.at[0], one_r.at[0], partner)
    pair = []
    for m, offset in enumerate(PAIR_ORDER):
        target = lax.rem(y + offset + 8, 8)
        pair.append(
            go(g_ref.at[:, target, 1 - c], pair_buf.at[m], pair_s.at[m], pair_r.at[m], partner)
        )
    edges = send_edges(space_ref, edge_ref, edge_s, edge_r, low, high)
    started.extend(edges)
    arrived = {}
    waited = set()

    def local(offset, k):
        m = PAIR_ORDER.index(offset)
        if m not in waited:
            pair[m].wait_recv()
            waited.add(m)
        return g_ref[k, lax.rem(y + offset + 8, 8), c] + pair_buf[m, k]

    for s in range(4):
        for k in range(2):
            for d in range(2):
                if s == 0 and k != d:
                    continue
                offset = 4 if s == 0 else (4 - s if d == 0 else s - 4)
                value = local(offset, k)
                if (d, k) in arrived:
                    arrived[d, k].wait_recv()
                    value = value + ring_dst[d, s - 1, k].astype(f32)
                ring_src[d, s, k] = value.astype(ring_src.dtype)
                arrived[d, k] = go(
                    ring_src.at[d, s, k],
                    ring_dst.at[d, s, k],
                    ring_s.at[d, s, k],
                    ring_r.at[d, s, k],
                    ring[d],
                )
        if s == 0:
            norm_pair.wait_recv()
            part = n_ref[...] + n_pair[...]
            n_y_src[...] = part
            n_y[y] = part
            norm_y = [
                go(n_y_src, n_y.at[y], ny_s.at[i], ny_r.at[i], peer)
                for i, peer in enumerate(y_peers)
            ]
        if s == 1:
            for copy in norm_y:
                copy.wait_recv()
            part = n_y[0]
            for i in range(1, 8):
                part = part + n_y[i]
            n_x_src[...] = part
            norm_x = go(n_x_src, n_x, one_s.at[1], one_r.at[1], across)
        if s == 2:
            norm_x.wait_recv()
            part = n_x_src[...] + n_x[...]
            n_z_src[...] = part
            n_z[z] = part
            norm_z = [
                go(n_z_src, n_z.at[z], nz_s.at[i], nz_r.at[i], peer)
                for i, peer in enumerate(z_peers)
            ]
        if s == 3:
            for copy in norm_z:
                copy.wait_recv()
            part = n_z[0]
            for i in range(1, 8):
                part = part + n_z[i]
            n_h_src[...] = part
            norm_h = go(n_h_src, n_h, one_s.at[2], one_r.at[2], far)

    totals = []
    for k in range(2):
        value = local(0, k)
        for d in range(2):
            arrived[d, k].wait_recv()
            value = value + ring_dst[d, 3, k].astype(f32)
        totals.append(value)
    keep = jnp.where(x == 0, totals[0], totals[1])
    x_src[...] = jnp.where(x == 0, totals[1], totals[0])
    x_copy = go(x_src, x_dst, one_s.at[3], one_r.at[3], across)
    x_copy.wait_recv()
    value = keep + x_dst[...]
    for p in range(8):
        held[p] = value[(p // 2) * 24 : (p // 2) * 24 + 24, (p % 2) * 128 : (p % 2) * 128 + 128]
    scatter = [
        go(held.at[lax.rem(z + i + 1, 8)], z_dst.at[z], zs_s.at[i], zs_r.at[i], peer)
        for i, peer in enumerate(z_peers)
    ]
    z_dst[z] = held[z]
    for copy in scatter:
        copy.wait_recv()
    part = z_dst[0]
    for i in range(1, 8):
        part = part + z_dst[i]
    h_src[...] = part
    h_copy = go(h_src, h_dst, one_s.at[4], one_r.at[4], far)
    norm_h.wait_recv()
    norm_ref[...] = n_h_src[...] + n_h[...]
    h_copy.wait_recv()
    part = h_src[...] + h_dst[...]
    z_src[...] = part
    out_ref[z] = part
    spread = [
        go(z_src, out_ref.at[z], zg_s.at[i], zg_r.at[i], peer) for i, peer in enumerate(z_peers)
    ]
    for copy in spread + edges:
        copy.wait_recv()
    for copy in started:
        copy.wait_send()


def reduce_gradient(gradient, norms, space):
    f32, bf16 = jnp.float32, jnp.bfloat16
    dma, vmem = pltpu.SemaphoreType.DMA, pltpu.VMEM
    small = vmem((8, 128), f32)
    eight = vmem((8, 8, 128), f32)
    return pl.pallas_call(
        reduce_kernel,
        out_shape=(
            jax.ShapeDtypeStruct((8, 24, 128), f32),
            jax.ShapeDtypeStruct((8, 128), f32),
            jax.ShapeDtypeStruct(space.shape, space.dtype),
        ),
        in_specs=[VMEM, VMEM, VMEM],
        out_specs=(VMEM, VMEM, VMEM),
        scratch_shapes=[
            vmem((8, 2, 96, 256), f32),
            vmem((2, 4, 2, 96, 256), bf16),
            vmem((2, 4, 2, 96, 256), bf16),
            vmem((96, 256), f32),
            vmem((96, 256), f32),
            vmem((8, 24, 128), f32),
            vmem((8, 24, 128), f32),
            vmem((24, 128), f32),
            vmem((24, 128), f32),
            vmem((24, 128), f32),
            small,
            small,
            eight,
            small,
            small,
            small,
            eight,
            small,
            small,
            dma((8,)),
            dma((8,)),
            dma((2, 4, 2)),
            dma((2, 4, 2)),
            dma((7,)),
            dma((7,)),
            dma((7,)),
            dma((7,)),
            dma((5,)),
            dma((5,)),
            dma((7,)),
            dma((7,)),
            dma((7,)),
            dma((7,)),
            dma((2,)),
            dma((2,)),
        ],
        compiler_params=pltpu.CompilerParams(
            collective_id=1, has_side_effects=True, vmem_limit_bytes=40 * 2**20
        ),
        name="reduce_gradient",
    )(gradient.reshape(2, 8, 2, 96, 256), norms, space)


PITCH = 48
ROWS = 16 * PITCH
TALL = ROWS + 2 * PITCH
CHUNK = 2 * PITCH


def group_mean(row):
    rows = lax.broadcasted_iota(jnp.int32, (256, 256), 0) // 8
    columns = lax.broadcasted_iota(jnp.int32, (256, 256), 1) // 8
    same = (rows == columns).astype(jnp.float32)
    total = jnp.dot(
        jnp.broadcast_to(row, (8, 256)),
        same,
        precision=lax.Precision.HIGHEST,
        preferred_element_type=jnp.float32,
    )
    return total[0:1] * (1.0 / (16 * 36 * 8))


def block_kernel(
    clip_ref,
    cot_ref,
    edge_ref,
    w_ref,
    gain_ref,
    bias_ref,
    space_ref,
    input_ref,
    g_ref,
    norm_ref,
    cot_pad,
    wide,
    tall,
    hat,
    back,
    act,
    grad,
    flip,
    space,
):
    f32, bf16 = jnp.float32, jnp.bfloat16
    t = lax.axis_index("tm")
    gain, bias = gain_ref[...], bias_ref[...]
    inside = (lax.broadcasted_iota(jnp.int32, (2, PITCH, 256), 1) < 36).reshape(CHUNK, 256)

    def dot(a, b, contract=(1, 0)):
        dims = (((contract[0],), (contract[1],)), ((), ()))
        return lax.dot_general(a, b, dims, preferred_element_type=f32)

    def shift(target, f):
        for j in range(3):
            for start in range(0, TALL, CHUNK):
                target[f, start : start + CHUNK, j * 256 : (j + 1) * 256] = tall[
                    start + 7 + j : start + 7 + j + CHUNK
                ].astype(bf16)

    cot_pad[...] = jnp.zeros_like(cot_pad)
    wide[...] = jnp.zeros_like(wide)
    tall[...] = jnp.zeros_like(tall)
    cot_pad[0, :, :36] = jnp.where(t == 0, 0.0, edge_ref[0].astype(f32)).astype(bf16)
    cot_pad[1, :, :36] = cot_ref[0]
    cot_pad[2, :, :36] = cot_ref[1]
    cot_pad[3, :, :36] = jnp.where(t == 15, 0.0, edge_ref[1].astype(f32)).astype(bf16)
    for i in range(3):
        for j in range(3):
            tap = 3 * i + j
            slot = 3 * i + 2 - j
            flip[slot * 256 : (slot + 1) * 256] = w_ref[tap * 256 : (tap + 1) * 256].T

    def body(start):
        return pl.ds(pl.multiple_of(start * CHUNK, CHUNK), CHUNK)

    def above(start):
        return pl.ds(pl.multiple_of(start * CHUNK + PITCH + 8, 8), CHUNK)

    def folded(value):
        return jnp.sum(value.reshape(CHUNK // 8, 8, 256), axis=0)

    def field(i):
        return wide[pl.ds(i * 2, 2)].reshape(CHUNK, 256)

    zero = jnp.zeros((8, 256), f32)
    inverse = []
    for f in range(2):
        wide[:, :36] = clip_ref[f].astype(f32)
        total = lax.fori_loop(0, 8, lambda i, carry: carry + folded(field(i)), zero)
        center = group_mean(jnp.sum(total, axis=0, keepdims=True))

        def squares(i, carry):
            value = jnp.where(inside, field(i) - center, 0.0)
            return carry + folded(value * value)

        total = lax.fori_loop(0, 8, squares, zero)
        spread = group_mean(jnp.sum(total, axis=0, keepdims=True))
        scale = lax.rsqrt(spread + 1e-05)
        inverse.append(scale)

        def activate(i, carry):
            normed = jnp.where(inside, (field(i) - center) * scale, 0.0)
            hat[f, body(i)] = normed
            u = normed * gain + bias
            value = jnp.where(inside, u / (1.0 + jnp.exp(-u)), 0.0)
            tall[above(i)] = value
            return carry

        lax.fori_loop(0, 8, activate, 0)
        shift(act, f)

    for f in range(2):
        total = dot(act[f, 0:ROWS], w_ref[0:768])
        for i in range(1, 3):
            total = total + dot(act[f, i * PITCH : i * PITCH + ROWS], w_ref[i * 768 : (i + 1) * 768])
        rounded = total.astype(bf16)
        space[f] = rounded
        space_ref[f] = rounded.reshape(16, PITCH, 256)[:, :36]

    for f in range(2):
        total = None
        for k in range(3):
            tap = w_ref[(9 + k) * 256 : (10 + k) * 256]
            term = dot(cot_pad[f + 2 - k].reshape(ROWS, 256), tap, (1, 1))
            total = term if total is None else total + term
        tall[PITCH + 8 : PITCH + 8 + ROWS] = total.astype(bf16).astype(f32)
        shift(grad, f)

    for k in range(3):
        total = None
        for f in range(2):
            term = dot(space[f], cot_pad[f + 2 - k].reshape(ROWS, 256), (0, 0))
            total = term if total is None else total + term
        g_ref[(9 + k) * 256 : (10 + k) * 256] = total
    for i in range(3):
        total = None
        for f in range(2):
            term = dot(
                act[f, i * PITCH : i * PITCH + ROWS],
                grad[f, PITCH : PITCH + ROWS, 256:512],
                (0, 0),
            )
            total = term if total is None else total + term
        g_ref[i * 768 : (i + 1) * 768] = total

    gain_sum, bias_sum = zero, zero
    for f in range(2):
        total = None
        for i in range(3):
            low = (2 - i) * PITCH
            term = dot(grad[f, low : low + ROWS], flip[i * 768 : (i + 1) * 768])
            total = term if total is None else total + term
        back[...] = total

        def pull(i, carry):
            normed = hat[f, body(i)]
            u = normed * gain + bias
            gate = 1.0 / (1.0 + jnp.exp(-u))
            down = jnp.where(inside, back[body(i)] * (gate * (1.0 + u * (1.0 - gate))), 0.0)
            back[body(i)] = down
            return carry[0] + folded(down), carry[1] + folded(down * normed)

        plain, weighted = lax.fori_loop(0, 8, pull, (zero, zero))
        bias_sum, gain_sum = bias_sum + plain, gain_sum + weighted
        plain = group_mean(gain * jnp.sum(plain, axis=0, keepdims=True))
        weighted = group_mean(gain * jnp.sum(weighted, axis=0, keepdims=True))
        scale = inverse[f]

        def finish(i, carry):
            term = scale * (back[body(i)] * gain - plain - hat[f, body(i)] * weighted)
            pair = cot_pad[f + 1, pl.ds(i * 2, 2)].reshape(CHUNK, 256)
            result = (pair.astype(f32) + term).reshape(2, PITCH, 256)[:, :36]
            input_ref[f, pl.ds(i * 2, 2)] = result.astype(bf16)
            return carry

        lax.fori_loop(0, 8, finish, 0)
    norm_ref[0:1] = jnp.sum(gain_sum, axis=0, keepdims=True)
    norm_ref[1:2] = jnp.sum(bias_sum, axis=0, keepdims=True)


def block(clips, cotangent, edges, weights, gain, bias):
    f32, bf16 = jnp.float32, jnp.bfloat16
    vmem = pltpu.VMEM
    return pl.pallas_call(
        block_kernel,
        out_shape=(
            jax.ShapeDtypeStruct(clips.shape, bf16),
            jax.ShapeDtypeStruct(clips.shape, bf16),
            jax.ShapeDtypeStruct(weights.shape, f32),
            jax.ShapeDtypeStruct((2, 256), f32),
        ),
        in_specs=[VMEM] * 6,
        out_specs=(VMEM,) * 4,
        scratch_shapes=[
            vmem((4, 16, PITCH, 256), bf16),
            vmem((16, PITCH, 256), f32),
            vmem((TALL + 16, 256), f32),
            vmem((2, ROWS, 256), f32),
            vmem((ROWS, 256), f32),
            vmem((2, TALL, 768), bf16),
            vmem((2, TALL, 768), bf16),
            vmem((2304, 256), bf16),
            vmem((2, ROWS, 256), bf16),
        ],
        compiler_params=pltpu.CompilerParams(vmem_limit_bytes=56 * 2**20),
        name="block",
    )(clips, cotangent, edges, weights, gain.reshape(1, 256), bias.reshape(1, 256))


def shards(clips, cotangent, conv_master, first_moment, second_moment, norm_gain, norm_bias):
    f32 = jnp.float32
    channels = clips.shape[-1]
    clip, cot = clips[0], cotangent[0]
    rows, edges = gather_weights(conv_master.astype(jnp.bfloat16), cot)
    weights = rows.reshape(12 * channels, channels)
    space, input_grad, local_gradient, norms = block(
        clip, cot, edges, weights, norm_gain, norm_bias
    )
    norms = jnp.pad(norms.reshape(4, 128), ((0, 4), (0, 0)))
    pieces, norm_sums, around = reduce_gradient(local_gradient, norms, space)
    norm_grads = norm_sums[:4].reshape(2, channels)
    gradient = pieces.reshape(4, 2, 24, 128).transpose(0, 2, 1, 3).reshape(96, channels)
    t = lax.axis_index("tm")
    zero = jnp.zeros_like(around[:1])
    padded = jnp.concatenate(
        [
            jnp.where(t == 0, zero, around[:1]),
            space,
            jnp.where(t == lax.axis_size("tm") - 1, zero, around[1:]),
        ]
    )
    temporal = clip.astype(f32)
    for frame_tap in range(3):
        tap = weights[(9 + frame_tap) * channels : (10 + frame_tap) * channels]
        temporal = temporal + jnp.einsum(
            "fhwc,cd->fhwd",
            padded[frame_tap : frame_tap + 2],
            tap,
            preferred_element_type=f32,
        )
    block_out = temporal.astype(jnp.bfloat16)[None]
    input_grad = input_grad[None]
    new_master, new_first, new_second = adam_update(
        gradient, conv_master, first_moment, second_moment
    )
    return (block_out, input_grad, new_master, new_first, new_second, norm_grads)


def solution(mesh):
    placed = (
        P("blk", "tm", None, None, None),
        P("blk", "tm", None, None, None),
        P("blk", None),
        P("blk", None),
        P("blk", None),
        P(),
        P(),
    )
    return jax.shard_map(
        shards,
        mesh=mesh,
        in_specs=placed,
        out_specs=(
            P("blk", "tm", None, None, None),
            P("blk", "tm", None, None, None),
            P("blk", None),
            P("blk", None),
            P("blk", None),
            P(),
        ),
        check_vma=False,
    )
```

```python
import jax
import jax.numpy as jnp
from jax import lax
from jax.experimental import pallas as pl
from jax.experimental.pallas import tpu as pltpu
from jax.sharding import PartitionSpec as P


beta_one = 0.9
beta_two = 0.999
learn_rate = 0.003
adam_eps = 1e-08
bias_first = 1.0 - 0.9**10
bias_second = 1.0 - 0.999**10


def adam_update(gradient, master, first, second):
    new_first = beta_one * first + (1.0 - beta_one) * gradient
    new_second = beta_two * second + (1.0 - beta_two) * gradient * gradient
    update = new_first / bias_first / (jnp.sqrt(new_second / bias_second) + adam_eps)
    return (master - learn_rate * update, new_first, new_second)

MESH = pl.DeviceIdType.MESH
VMEM = pl.BlockSpec(memory_space=pltpu.VMEM)


def place():
    me = lax.axis_index("blk")
    return me // 16, lax.rem(me // 2, 8), lax.rem(me, 2), lax.axis_index("tm")


def owner(x, y, c):
    return x * 16 + lax.rem(y + 8, 8) * 2 + c


def greet(peers):
    barrier = pltpu.get_barrier_semaphore()
    for peer in peers:
        pl.semaphore_signal(barrier, inc=1, device_id=peer, device_id_type=MESH)
    pl.semaphore_wait(barrier, len(peers))


def send(src, dst, send_sem, recv_sem, peer):
    copy = pltpu.make_async_remote_copy(
        src_ref=src,
        dst_ref=dst,
        send_sem=send_sem,
        recv_sem=recv_sem,
        device_id=peer,
        device_id_type=MESH,
    )
    copy.start()
    return copy


def at_chip(position, y, c, t):
    position = lax.rem(position + 4, 4)
    t = lax.rem(t + 16, 16)
    return owner(lax.rem(position, 2), y, c), (t // 2) * 2 + position // 2


class Edges:
    def __init__(self, frames, edges, relay, sems):
        self.frames, self.edges, self.relay, self.sems = frames, edges, relay, sems
        x, y, c, t = place()
        here = lax.rem(t, 2) * 2 + x
        self.near, self.last, self.source = [], [], []
        for step in (1, -1):
            z = t // 2
            origin = lax.rem(here - step + 4, 4)
            t_origin = z * 2 + origin // 2
            t_last = lax.rem(t_origin + step + 16, 16)
            self.near.append(at_chip(here + step, y, c, t))
            self.last.append((owner(lax.rem(origin, 2), y, c), t_last))
            self.source.append(at_chip(here - step, y, c, t - step))

    def signalled(self):
        return self.near + self.source

    def start(self):
        first_s, first_r, _, _ = self.sems
        self.first, self.second = {}, []
        for q in range(4):
            for d in range(2):
                rows = pl.ds(q * 4, 4)
                self.first[d, q] = send(
                    self.frames.at[1 - d, rows],
                    self.relay.at[d, rows],
                    first_s.at[d, q],
                    first_r.at[d, q],
                    self.near[d],
                )

    def forward(self, q):
        _, _, second_s, second_r = self.sems
        for d in range(2):
            rows = pl.ds(q * 4, 4)
            self.first[d, q].wait_recv()
            self.second.append(
                send(
                    self.relay.at[d, rows],
                    self.edges.at[d, rows],
                    second_s.at[d, q],
                    second_r.at[d, q],
                    self.last[d],
                )
            )

    def finish(self):
        for copy in self.second:
            copy.wait()
        for copy in self.first.values():
            copy.wait_send()


def edge_scratch(frames):
    dma = pltpu.SemaphoreType.DMA
    return [pltpu.VMEM(frames.shape, frames.dtype)] + [dma((2, 4))] * 4


def gather_kernel(
    w_ref,
    cot_ref,
    out_ref,
    edge_ref,
    ring_send,
    ring_recv,
    pair_send,
    pair_recv,
    x_send,
    x_recv,
    relay,
    *edge_sems,
):
    x, y, c, t = place()
    partner = (owner(x, y, 1 - c), t)
    across = (owner(1 - x, y, c), t)
    ring = ((owner(x, y + 1, c), t), (owner(x, y - 1, c), t))
    edges = Edges(cot_ref, edge_ref, relay, edge_sems)
    greet([partner, across, ring[0], ring[1]] + edges.signalled())
    started = []

    def pass_on(src, k, offset):
        slot = k * 8 + offset % 8
        dst = out_ref.at[owner(x if k == 0 else 1 - x, y + offset, c)]
        started.append(send(src, dst, pair_send.at[slot], pair_recv.at[slot], partner))

    def hop(src, d, s, k):
        offset = -s if d == 0 else s
        dst = out_ref.at[owner(x if k == 0 else 1 - x, y + offset, c)]
        copy = send(src, dst, ring_send.at[d, s, k], ring_recv.at[d, s, k], ring[d])
        started.append(copy)
        return copy

    mine = owner(x, y, c)
    x_copy = send(w_ref, out_ref.at[mine], x_send, x_recv, across)
    copies = {}
    for d in range(2):
        copies[d, 0] = hop(w_ref, d, 0, 0)
    pass_on(w_ref, 0, 0)
    edges.start()
    out_ref[mine] = w_ref[...]
    x_copy.wait_recv()
    other = out_ref.at[owner(1 - x, y, c)]
    for d in range(2):
        copies[d, 1] = hop(other, d, 0, 1)
    pass_on(other, 1, 0)
    for s in range(1, 5):
        for k in range(2):
            for d in range(2):
                if s == 4 and k != d:
                    continue
                offset = -s if d == 0 else s
                copies[d, k].wait_recv()
                block = out_ref.at[owner(x if k == 0 else 1 - x, y + offset, c)]
                if s < 3 or (s == 3 and k == d):
                    copies[d, k] = hop(block, d, s, k)
                pass_on(block, k, offset)
        edges.forward(s - 1)
    x_copy.wait_send()
    for copy in started:
        copy.wait_send()
    for slot in range(16):
        k, offset = slot // 8, slot % 8
        block = out_ref.at[owner(x if k == 0 else 1 - x, y + offset, 1 - c)]
        pltpu.make_async_remote_copy(
            src_ref=w_ref,
            dst_ref=block,
            send_sem=pair_send.at[slot],
            recv_sem=pair_recv.at[slot],
            device_id=partner,
            device_id_type=MESH,
        ).wait_recv()
    edges.finish()


def gather_weights(rows, cotangent):
    dma = pltpu.SemaphoreType.DMA
    return pl.pallas_call(
        gather_kernel,
        out_shape=(
            jax.ShapeDtypeStruct((32,) + rows.shape, rows.dtype),
            jax.ShapeDtypeStruct(cotangent.shape, cotangent.dtype),
        ),
        in_specs=[VMEM, VMEM],
        out_specs=(VMEM, VMEM),
        scratch_shapes=[
            dma((2, 4, 2)),
            dma((2, 4, 2)),
            dma((16,)),
            dma((16,)),
            dma(()),
            dma(()),
        ]
        + edge_scratch(cotangent),
        compiler_params=pltpu.CompilerParams(
            collective_id=0, has_side_effects=True, vmem_limit_bytes=10 * 2**20
        ),
        name="gather_weights",
    )(rows, cotangent)


PAIR_ORDER = (4, 3, -3, 2, -2, 1, -1, 0)


def reduce_kernel(
    g_ref,
    n_ref,
    space_ref,
    out_ref,
    norm_ref,
    edge_ref,
    pair_buf,
    ring_src,
    ring_dst,
    x_src,
    x_dst,
    held,
    z_dst,
    h_src,
    h_dst,
    z_src,
    n_pair,
    n_y_src,
    n_y,
    n_x_src,
    n_x,
    n_z_src,
    n_z,
    n_h_src,
    n_h,
    pair_s,
    pair_r,
    ring_s,
    ring_r,
    zs_s,
    zs_r,
    zg_s,
    zg_r,
    one_s,
    one_r,
    ny_s,
    ny_r,
    nz_s,
    nz_r,
    relay,
    *edge_sems,
):
    f32 = jnp.float32
    x, y, c, t = place()
    z, h = t // 2, lax.rem(t, 2)
    mine = owner(x, y, c)
    partner = (owner(x, y, 1 - c), t)
    across = (owner(1 - x, y, c), t)
    far = (mine, z * 2 + 1 - h)
    y_peers = [(owner(x, y + i, c), t) for i in range(1, 8)]
    z_peers = [(mine, lax.rem(z + i, 8) * 2 + h) for i in range(1, 8)]
    ring = (y_peers[0], y_peers[6])
    edges = Edges(space_ref, edge_ref, relay, edge_sems)
    greet([partner, across, far] + y_peers + z_peers + edges.signalled())
    started = []

    def go(*args):
        copy = send(*args)
        started.append(copy)
        return copy

    norm_pair = go(n_ref, n_pair, one_s.at[0], one_r.at[0], partner)
    pair = []
    for m, offset in enumerate(PAIR_ORDER):
        target = lax.rem(y + offset + 8, 8)
        pair.append(
            go(g_ref.at[:, target, 1 - c], pair_buf.at[m], pair_s.at[m], pair_r.at[m], partner)
        )
    edges.start()
    arrived = {}
    waited = set()

    def local(offset, k):
        m = PAIR_ORDER.index(offset)
        if m not in waited:
            pair[m].wait_recv()
            waited.add(m)
        return g_ref[k, lax.rem(y + offset + 8, 8), c] + pair_buf[m, k]

    for s in range(4):
        for k in range(2):
            for d in range(2):
                if s == 0 and k != d:
                    continue
                offset = 4 if s == 0 else (4 - s if d == 0 else s - 4)
                value = local(offset, k)
                if (d, k) in arrived:
                    arrived[d, k].wait_recv()
                    value = value + ring_dst[d, s - 1, k].astype(f32)
                ring_src[d, s, k] = value.astype(ring_src.dtype)
                arrived[d, k] = go(
                    ring_src.at[d, s, k],
                    ring_dst.at[d, s, k],
                    ring_s.at[d, s, k],
                    ring_r.at[d, s, k],
                    ring[d],
                )
        if s == 0:
            norm_pair.wait_recv()
            part = n_ref[...] + n_pair[...]
            n_y_src[...] = part
            n_y[y] = part
            norm_y = [
                go(n_y_src, n_y.at[y], ny_s.at[i], ny_r.at[i], peer)
                for i, peer in enumerate(y_peers)
            ]
        if s == 1:
            for copy in norm_y:
                copy.wait_recv()
            part = n_y[0]
            for i in range(1, 8):
                part = part + n_y[i]
            n_x_src[...] = part
            norm_x = go(n_x_src, n_x, one_s.at[1], one_r.at[1], across)
        if s == 2:
            norm_x.wait_recv()
            part = n_x_src[...] + n_x[...]
            n_z_src[...] = part
            n_z[z] = part
            norm_z = [
                go(n_z_src, n_z.at[z], nz_s.at[i], nz_r.at[i], peer)
                for i, peer in enumerate(z_peers)
            ]
        if s == 3:
            for copy in norm_z:
                copy.wait_recv()
            part = n_z[0]
            for i in range(1, 8):
                part = part + n_z[i]
            n_h_src[...] = part
            norm_h = go(n_h_src, n_h, one_s.at[2], one_r.at[2], far)
        edges.forward(s)

    totals = []
    for k in range(2):
        value = local(0, k)
        for d in range(2):
            arrived[d, k].wait_recv()
            value = value + ring_dst[d, 3, k].astype(f32)
        totals.append(value)
    keep = jnp.where(x == 0, totals[0], totals[1])
    x_src[...] = jnp.where(x == 0, totals[1], totals[0])
    x_copy = go(x_src, x_dst, one_s.at[3], one_r.at[3], across)
    x_copy.wait_recv()
    value = keep + x_dst[...]
    for p in range(8):
        held[p] = value[(p // 2) * 24 : (p // 2) * 24 + 24, (p % 2) * 128 : (p % 2) * 128 + 128]
    scatter = [
        go(held.at[lax.rem(z + i + 1, 8)], z_dst.at[z], zs_s.at[i], zs_r.at[i], peer)
        for i, peer in enumerate(z_peers)
    ]
    z_dst[z] = held[z]
    for copy in scatter:
        copy.wait_recv()
    part = z_dst[0]
    for i in range(1, 8):
        part = part + z_dst[i]
    h_src[...] = part
    h_copy = go(h_src, h_dst, one_s.at[4], one_r.at[4], far)
    norm_h.wait_recv()
    norm_ref[...] = n_h_src[...] + n_h[...]
    h_copy.wait_recv()
    part = h_src[...] + h_dst[...]
    z_src[...] = part
    out_ref[z] = part
    spread = [
        go(z_src, out_ref.at[z], zg_s.at[i], zg_r.at[i], peer) for i, peer in enumerate(z_peers)
    ]
    for copy in spread:
        copy.wait_recv()
    edges.finish()
    for copy in started:
        copy.wait_send()


def reduce_gradient(gradient, norms, space):
    f32, bf16 = jnp.float32, jnp.bfloat16
    dma, vmem = pltpu.SemaphoreType.DMA, pltpu.VMEM
    small = vmem((8, 128), f32)
    eight = vmem((8, 8, 128), f32)
    return pl.pallas_call(
        reduce_kernel,
        out_shape=(
            jax.ShapeDtypeStruct((8, 24, 128), f32),
            jax.ShapeDtypeStruct((8, 128), f32),
            jax.ShapeDtypeStruct(space.shape, space.dtype),
        ),
        in_specs=[VMEM, VMEM, VMEM],
        out_specs=(VMEM, VMEM, VMEM),
        scratch_shapes=[
            vmem((8, 2, 96, 256), f32),
            vmem((2, 4, 2, 96, 256), bf16),
            vmem((2, 4, 2, 96, 256), bf16),
            vmem((96, 256), f32),
            vmem((96, 256), f32),
            vmem((8, 24, 128), f32),
            vmem((8, 24, 128), f32),
            vmem((24, 128), f32),
            vmem((24, 128), f32),
            vmem((24, 128), f32),
            small,
            small,
            eight,
            small,
            small,
            small,
            eight,
            small,
            small,
            dma((8,)),
            dma((8,)),
            dma((2, 4, 2)),
            dma((2, 4, 2)),
            dma((7,)),
            dma((7,)),
            dma((7,)),
            dma((7,)),
            dma((5,)),
            dma((5,)),
            dma((7,)),
            dma((7,)),
            dma((7,)),
            dma((7,)),
        ]
        + edge_scratch(space),
        compiler_params=pltpu.CompilerParams(
            collective_id=1, has_side_effects=True, vmem_limit_bytes=18 * 2**20
        ),
        name="reduce_gradient",
    )(gradient.reshape(2, 8, 2, 96, 256), norms, space)


PITCH = 48
ROWS = 16 * PITCH
TALL = ROWS + 2 * PITCH
CHUNK = 2 * PITCH


def group_mean(row):
    rows = lax.broadcasted_iota(jnp.int32, (256, 256), 0) // 8
    columns = lax.broadcasted_iota(jnp.int32, (256, 256), 1) // 8
    same = (rows == columns).astype(jnp.float32)
    total = jnp.dot(
        jnp.broadcast_to(row, (8, 256)),
        same,
        precision=lax.Precision.HIGHEST,
        preferred_element_type=jnp.float32,
    )
    return total[0:1] * (1.0 / (16 * 36 * 8))


def block_kernel(
    clip_ref,
    cot_ref,
    edge_ref,
    w_ref,
    gain_ref,
    bias_ref,
    space_ref,
    input_ref,
    g_ref,
    norm_ref,
    cot_pad,
    wide,
    tall,
    hat,
    back,
    act,
    grad,
    flip,
    space,
):
    f32, bf16 = jnp.float32, jnp.bfloat16
    t = lax.axis_index("tm")
    gain, bias = gain_ref[...], bias_ref[...]
    inside = (lax.broadcasted_iota(jnp.int32, (2, PITCH, 256), 1) < 36).reshape(CHUNK, 256)

    def dot(a, b, contract=(1, 0)):
        dims = (((contract[0],), (contract[1],)), ((), ()))
        return lax.dot_general(a, b, dims, preferred_element_type=f32)

    def shift(target, f):
        for j in range(3):
            for start in range(0, TALL, CHUNK):
                target[f, start : start + CHUNK, j * 256 : (j + 1) * 256] = tall[
                    start + 7 + j : start + 7 + j + CHUNK
                ].astype(bf16)

    cot_pad[...] = jnp.zeros_like(cot_pad)
    wide[...] = jnp.zeros_like(wide)
    tall[...] = jnp.zeros_like(tall)
    cot_pad[0, :, :36] = jnp.where(t == 0, 0.0, edge_ref[0].astype(f32)).astype(bf16)
    cot_pad[1, :, :36] = cot_ref[0]
    cot_pad[2, :, :36] = cot_ref[1]
    cot_pad[3, :, :36] = jnp.where(t == 15, 0.0, edge_ref[1].astype(f32)).astype(bf16)
    for i in range(3):
        for j in range(3):
            tap = 3 * i + j
            slot = 3 * i + 2 - j
            flip[slot * 256 : (slot + 1) * 256] = w_ref[tap * 256 : (tap + 1) * 256].T

    def body(start):
        return pl.ds(pl.multiple_of(start * CHUNK, CHUNK), CHUNK)

    def above(start):
        return pl.ds(pl.multiple_of(start * CHUNK + PITCH + 8, 8), CHUNK)

    def folded(value):
        return jnp.sum(value.reshape(CHUNK // 8, 8, 256), axis=0)

    def field(i):
        return wide[pl.ds(i * 2, 2)].reshape(CHUNK, 256)

    zero = jnp.zeros((8, 256), f32)
    inverse = []
    for f in range(2):
        wide[:, :36] = clip_ref[f].astype(f32)
        total = lax.fori_loop(0, 8, lambda i, carry: carry + folded(field(i)), zero)
        center = group_mean(jnp.sum(total, axis=0, keepdims=True))

        def squares(i, carry):
            value = jnp.where(inside, field(i) - center, 0.0)
            return carry + folded(value * value)

        total = lax.fori_loop(0, 8, squares, zero)
        spread = group_mean(jnp.sum(total, axis=0, keepdims=True))
        scale = lax.rsqrt(spread + 1e-05)
        inverse.append(scale)

        def activate(i, carry):
            normed = jnp.where(inside, (field(i) - center) * scale, 0.0)
            hat[f, body(i)] = normed
            u = normed * gain + bias
            value = jnp.where(inside, u / (1.0 + jnp.exp(-u)), 0.0)
            tall[above(i)] = value
            return carry

        lax.fori_loop(0, 8, activate, 0)
        shift(act, f)

    for f in range(2):
        total = dot(act[f, 0:ROWS], w_ref[0:768])
        for i in range(1, 3):
            total = total + dot(act[f, i * PITCH : i * PITCH + ROWS], w_ref[i * 768 : (i + 1) * 768])
        rounded = total.astype(bf16)
        space[f] = rounded
        space_ref[f] = rounded.reshape(16, PITCH, 256)[:, :36]

    for f in range(2):
        total = None
        for k in range(3):
            tap = w_ref[(9 + k) * 256 : (10 + k) * 256]
            term = dot(cot_pad[f + 2 - k].reshape(ROWS, 256), tap, (1, 1))
            total = term if total is None else total + term
        tall[PITCH + 8 : PITCH + 8 + ROWS] = total.astype(bf16).astype(f32)
        shift(grad, f)

    for k in range(3):
        total = None
        for f in range(2):
            term = dot(space[f], cot_pad[f + 2 - k].reshape(ROWS, 256), (0, 0))
            total = term if total is None else total + term
        g_ref[(9 + k) * 256 : (10 + k) * 256] = total
    for i in range(3):
        total = None
        for f in range(2):
            term = dot(
                act[f, i * PITCH : i * PITCH + ROWS],
                grad[f, PITCH : PITCH + ROWS, 256:512],
                (0, 0),
            )
            total = term if total is None else total + term
        g_ref[i * 768 : (i + 1) * 768] = total

    gain_sum, bias_sum = zero, zero
    for f in range(2):
        total = None
        for i in range(3):
            low = (2 - i) * PITCH
            term = dot(grad[f, low : low + ROWS], flip[i * 768 : (i + 1) * 768])
            total = term if total is None else total + term
        back[...] = total

        def pull(i, carry):
            normed = hat[f, body(i)]
            u = normed * gain + bias
            gate = 1.0 / (1.0 + jnp.exp(-u))
            down = jnp.where(inside, back[body(i)] * (gate * (1.0 + u * (1.0 - gate))), 0.0)
            back[body(i)] = down
            return carry[0] + folded(down), carry[1] + folded(down * normed)

        plain, weighted = lax.fori_loop(0, 8, pull, (zero, zero))
        bias_sum, gain_sum = bias_sum + plain, gain_sum + weighted
        plain = group_mean(gain * jnp.sum(plain, axis=0, keepdims=True))
        weighted = group_mean(gain * jnp.sum(weighted, axis=0, keepdims=True))
        scale = inverse[f]

        def finish(i, carry):
            term = scale * (back[body(i)] * gain - plain - hat[f, body(i)] * weighted)
            pair = cot_pad[f + 1, pl.ds(i * 2, 2)].reshape(CHUNK, 256)
            result = (pair.astype(f32) + term).reshape(2, PITCH, 256)[:, :36]
            input_ref[f, pl.ds(i * 2, 2)] = result.astype(bf16)
            return carry

        lax.fori_loop(0, 8, finish, 0)
    norm_ref[0:1] = jnp.sum(gain_sum, axis=0, keepdims=True)
    norm_ref[1:2] = jnp.sum(bias_sum, axis=0, keepdims=True)


def block(clips, cotangent, edges, weights, gain, bias):
    f32, bf16 = jnp.float32, jnp.bfloat16
    vmem = pltpu.VMEM
    return pl.pallas_call(
        block_kernel,
        out_shape=(
            jax.ShapeDtypeStruct(clips.shape, bf16),
            jax.ShapeDtypeStruct(clips.shape, bf16),
            jax.ShapeDtypeStruct(weights.shape, f32),
            jax.ShapeDtypeStruct((2, 256), f32),
        ),
        in_specs=[VMEM] * 6,
        out_specs=(VMEM,) * 4,
        scratch_shapes=[
            vmem((4, 16, PITCH, 256), bf16),
            vmem((16, PITCH, 256), f32),
            vmem((TALL + 16, 256), f32),
            vmem((2, ROWS, 256), f32),
            vmem((ROWS, 256), f32),
            vmem((2, TALL, 768), bf16),
            vmem((2, TALL, 768), bf16),
            vmem((2304, 256), bf16),
            vmem((2, ROWS, 256), bf16),
        ],
        compiler_params=pltpu.CompilerParams(vmem_limit_bytes=36 * 2**20),
        name="block",
    )(clips, cotangent, edges, weights, gain.reshape(1, 256), bias.reshape(1, 256))


def shards(clips, cotangent, conv_master, first_moment, second_moment, norm_gain, norm_bias):
    f32 = jnp.float32
    channels = clips.shape[-1]
    clip, cot = clips[0], cotangent[0]
    rows, edges = gather_weights(conv_master.astype(jnp.bfloat16), cot)
    weights = rows.reshape(12 * channels, channels)
    space, input_grad, local_gradient, norms = block(
        clip, cot, edges, weights, norm_gain, norm_bias
    )
    norms = jnp.pad(norms.reshape(4, 128), ((0, 4), (0, 0)))
    pieces, norm_sums, around = reduce_gradient(local_gradient, norms, space)
    norm_grads = norm_sums[:4].reshape(2, channels)
    gradient = pieces.reshape(4, 2, 24, 128).transpose(0, 2, 1, 3).reshape(96, channels)
    t = lax.axis_index("tm")
    zero = jnp.zeros_like(around[:1])
    padded = jnp.concatenate(
        [
            jnp.where(t == 0, zero, around[:1]),
            space,
            jnp.where(t == lax.axis_size("tm") - 1, zero, around[1:]),
        ]
    )
    temporal = clip.astype(f32)
    for frame_tap in range(3):
        tap = weights[(9 + frame_tap) * channels : (10 + frame_tap) * channels]
        temporal = temporal + jnp.einsum(
            "fhwc,cd->fhwd",
            padded[frame_tap : frame_tap + 2],
            tap,
            preferred_element_type=f32,
        )
    block_out = temporal.astype(jnp.bfloat16)[None]
    input_grad = input_grad[None]
    new_master, new_first, new_second = adam_update(
        gradient, conv_master, first_moment, second_moment
    )
    return (block_out, input_grad, new_master, new_first, new_second, norm_grads)


def solution(mesh):
    placed = (
        P("blk", "tm", None, None, None),
        P("blk", "tm", None, None, None),
        P("blk", None),
        P("blk", None),
        P("blk", None),
        P(),
        P(),
    )
    return jax.shard_map(
        shards,
        mesh=mesh,
        in_specs=placed,
        out_specs=(
            P("blk", "tm", None, None, None),
            P("blk", "tm", None, None, None),
            P("blk", None),
            P("blk", None),
            P("blk", None),
            P(),
        ),
        check_vma=False,
    )
```

```python
import jax
import jax.numpy as jnp
from jax import lax
from jax.experimental import pallas as pl
from jax.experimental.pallas import tpu as pltpu
from jax.sharding import PartitionSpec as P


beta_one = 0.9
beta_two = 0.999
learn_rate = 0.003
adam_eps = 1e-08
bias_first = 1.0 - 0.9**10
bias_second = 1.0 - 0.999**10


def adam_update(gradient, master, first, second):
    new_first = beta_one * first + (1.0 - beta_one) * gradient
    new_second = beta_two * second + (1.0 - beta_two) * gradient * gradient
    update = new_first / bias_first / (jnp.sqrt(new_second / bias_second) + adam_eps)
    return (master - learn_rate * update, new_first, new_second)

MESH = pl.DeviceIdType.MESH
VMEM = pl.BlockSpec(memory_space=pltpu.VMEM)


def place():
    me = lax.axis_index("blk")
    return me // 16, lax.rem(me // 2, 8), lax.rem(me, 2), lax.axis_index("tm")


def owner(x, y, c):
    return x * 16 + lax.rem(y + 8, 8) * 2 + c


def greet(peers):
    barrier = pltpu.get_barrier_semaphore()
    for peer in peers:
        pl.semaphore_signal(barrier, inc=1, device_id=peer, device_id_type=MESH)
    pl.semaphore_wait(barrier, len(peers))


def send(src, dst, send_sem, recv_sem, peer):
    copy = pltpu.make_async_remote_copy(
        src_ref=src,
        dst_ref=dst,
        send_sem=send_sem,
        recv_sem=recv_sem,
        device_id=peer,
        device_id_type=MESH,
    )
    copy.start()
    return copy


def at_chip(position, y, c, t):
    position = lax.rem(position + 4, 4)
    t = lax.rem(t + 16, 16)
    return owner(lax.rem(position, 2), y, c), (t // 2) * 2 + position // 2


class Edges:
    def __init__(self, frames, edges, relay, sems):
        self.frames, self.edges, self.relay, self.sems = frames, edges, relay, sems
        x, y, c, t = place()
        here = lax.rem(t, 2) * 2 + x
        self.near, self.last, self.source = [], [], []
        for step in (1, -1):
            z = t // 2
            origin = lax.rem(here - step + 4, 4)
            t_origin = z * 2 + origin // 2
            t_last = lax.rem(t_origin + step + 16, 16)
            self.near.append(at_chip(here + step, y, c, t))
            self.last.append((owner(lax.rem(origin, 2), y, c), t_last))
            self.source.append(at_chip(here - step, y, c, t - step))

    def signalled(self):
        return self.near + self.source

    def start(self):
        first_s, first_r, _, _ = self.sems
        self.first, self.second = {}, []
        for q in range(4):
            for d in range(2):
                rows = pl.ds(q * 4, 4)
                self.first[d, q] = send(
                    self.frames.at[1 - d, rows],
                    self.relay.at[d, rows],
                    first_s.at[d, q],
                    first_r.at[d, q],
                    self.near[d],
                )

    def forward(self, q):
        _, _, second_s, second_r = self.sems
        for d in range(2):
            rows = pl.ds(q * 4, 4)
            self.first[d, q].wait_recv()
            self.second.append(
                send(
                    self.relay.at[d, rows],
                    self.edges.at[d, rows],
                    second_s.at[d, q],
                    second_r.at[d, q],
                    self.last[d],
                )
            )

    def finish(self):
        for copy in self.second:
            copy.wait()
        for copy in self.first.values():
            copy.wait_send()


def edge_scratch(frames):
    dma = pltpu.SemaphoreType.DMA
    return [pltpu.VMEM(frames.shape, frames.dtype)] + [dma((2, 4))] * 4


def gather_kernel(
    w_ref,
    cot_ref,
    out_ref,
    edge_ref,
    ring_send,
    ring_recv,
    pair_send,
    pair_recv,
    x_send,
    x_recv,
    relay,
    *edge_sems,
):
    x, y, c, t = place()
    partner = (owner(x, y, 1 - c), t)
    across = (owner(1 - x, y, c), t)
    ring = ((owner(x, y + 1, c), t), (owner(x, y - 1, c), t))
    edges = Edges(cot_ref, edge_ref, relay, edge_sems)
    greet([partner, across, ring[0], ring[1]] + edges.signalled())
    started = []

    def pass_on(src, k, offset):
        slot = k * 8 + offset % 8
        dst = out_ref.at[owner(x if k == 0 else 1 - x, y + offset, c)]
        started.append(send(src, dst, pair_send.at[slot], pair_recv.at[slot], partner))

    def hop(src, d, s, k):
        offset = -s if d == 0 else s
        dst = out_ref.at[owner(x if k == 0 else 1 - x, y + offset, c)]
        copy = send(src, dst, ring_send.at[d, s, k], ring_recv.at[d, s, k], ring[d])
        started.append(copy)
        return copy

    mine = owner(x, y, c)
    x_copy = send(w_ref, out_ref.at[mine], x_send, x_recv, across)
    copies = {}
    for d in range(2):
        copies[d, 0] = hop(w_ref, d, 0, 0)
    pass_on(w_ref, 0, 0)
    edges.start()
    out_ref[mine] = w_ref[...]
    x_copy.wait_recv()
    other = out_ref.at[owner(1 - x, y, c)]
    for d in range(2):
        copies[d, 1] = hop(other, d, 0, 1)
    pass_on(other, 1, 0)
    for s in range(1, 5):
        for k in range(2):
            for d in range(2):
                if s == 4 and k != d:
                    continue
                offset = -s if d == 0 else s
                copies[d, k].wait_recv()
                block = out_ref.at[owner(x if k == 0 else 1 - x, y + offset, c)]
                if s < 3 or (s == 3 and k == d):
                    copies[d, k] = hop(block, d, s, k)
                pass_on(block, k, offset)
        edges.forward(s - 1)
    x_copy.wait_send()
    for copy in started:
        copy.wait_send()
    for slot in range(16):
        k, offset = slot // 8, slot % 8
        block = out_ref.at[owner(x if k == 0 else 1 - x, y + offset, 1 - c)]
        pltpu.make_async_remote_copy(
            src_ref=w_ref,
            dst_ref=block,
            send_sem=pair_send.at[slot],
            recv_sem=pair_recv.at[slot],
            device_id=partner,
            device_id_type=MESH,
        ).wait_recv()
    edges.finish()


def gather_weights(rows, cotangent):
    dma = pltpu.SemaphoreType.DMA
    return pl.pallas_call(
        gather_kernel,
        out_shape=(
            jax.ShapeDtypeStruct((32,) + rows.shape, rows.dtype),
            jax.ShapeDtypeStruct(cotangent.shape, cotangent.dtype),
        ),
        in_specs=[VMEM, VMEM],
        out_specs=(VMEM, VMEM),
        scratch_shapes=[
            dma((2, 4, 2)),
            dma((2, 4, 2)),
            dma((16,)),
            dma((16,)),
            dma(()),
            dma(()),
        ]
        + edge_scratch(cotangent),
        compiler_params=pltpu.CompilerParams(
            collective_id=0, has_side_effects=True, vmem_limit_bytes=10 * 2**20
        ),
        name="gather_weights",
    )(rows, cotangent)


PITCH = 48
ROWS = 16 * PITCH
TALL = ROWS + 2 * PITCH
CHUNK = 2 * PITCH


def group_mean(row):
    rows = lax.broadcasted_iota(jnp.int32, (256, 256), 0) // 8
    columns = lax.broadcasted_iota(jnp.int32, (256, 256), 1) // 8
    same = (rows == columns).astype(jnp.float32)
    total = jnp.dot(
        jnp.broadcast_to(row, (8, 256)),
        same,
        precision=lax.Precision.HIGHEST,
        preferred_element_type=jnp.float32,
    )
    return total[0:1] * (1.0 / (16 * 36 * 8))


def pull_back(
    f, cot_ref, grad_ref, flip_ref, hat_ref, scale_ref, gain_ref, bias_ref, input_ref, back, wide
):
    f32, bf16 = jnp.float32, jnp.bfloat16
    gain, bias = gain_ref[...], bias_ref[...]
    inside = (lax.broadcasted_iota(jnp.int32, (2, PITCH, 256), 1) < 36).reshape(CHUNK, 256)
    zero = jnp.zeros((8, 256), f32)
    total = None
    for i in range(3):
        low = (2 - i) * PITCH
        term = jnp.dot(
            grad_ref[f, low : low + ROWS],
            flip_ref[i * 768 : (i + 1) * 768],
            preferred_element_type=f32,
        )
        total = term if total is None else total + term
    back[...] = total
    wide[...] = jnp.zeros_like(wide)
    wide[:, :36] = cot_ref[f]

    def body(start):
        return pl.ds(pl.multiple_of(start * CHUNK, CHUNK), CHUNK)

    def folded(value):
        return jnp.sum(value.reshape(CHUNK // 8, 8, 256), axis=0)

    def pull(i, carry):
        normed = hat_ref[f, body(i)]
        u = normed * gain + bias
        gate = 1.0 / (1.0 + jnp.exp(-u))
        down = jnp.where(inside, back[body(i)] * (gate * (1.0 + u * (1.0 - gate))), 0.0)
        back[body(i)] = down
        return carry[0] + folded(down), carry[1] + folded(down * normed)

    plain, weighted = lax.fori_loop(0, 8, pull, (zero, zero))
    plain = jnp.sum(plain, axis=0, keepdims=True)
    weighted = jnp.sum(weighted, axis=0, keepdims=True)
    plain_mean, weighted_mean = group_mean(gain * plain), group_mean(gain * weighted)
    scale = scale_ref[f : f + 1]

    def finish(i, carry):
        term = scale * (back[body(i)] * gain - plain_mean - hat_ref[f, body(i)] * weighted_mean)
        pair = wide[pl.ds(i * 2, 2)].reshape(CHUNK, 256)
        result = (pair.astype(f32) + term).reshape(2, PITCH, 256)[:, :36]
        input_ref[f, pl.ds(i * 2, 2)] = result.astype(bf16)
        return carry

    lax.fori_loop(0, 8, finish, 0)
    return plain, weighted


PAIR_ORDER = (4, 3, -3, 2, -2, 1, -1, 0)


def reduce_kernel(
    g_ref,
    space_ref,
    cot_ref,
    grad_ref,
    flip_ref,
    hat_ref,
    scale_ref,
    gain_ref,
    bias_ref,
    out_ref,
    norm_ref,
    edge_ref,
    input_ref,
    back,
    wide,
    n_ref,
    pair_buf,
    ring_src,
    ring_dst,
    x_src,
    x_dst,
    held,
    z_dst,
    h_src,
    h_dst,
    z_src,
    n_pair,
    n_y_src,
    n_y,
    n_x_src,
    n_x,
    n_z_src,
    n_z,
    n_h_src,
    n_h,
    pair_s,
    pair_r,
    ring_s,
    ring_r,
    zs_s,
    zs_r,
    zg_s,
    zg_r,
    one_s,
    one_r,
    ny_s,
    ny_r,
    nz_s,
    nz_r,
    relay,
    *edge_sems,
):
    f32 = jnp.float32
    x, y, c, t = place()
    z, h = t // 2, lax.rem(t, 2)
    mine = owner(x, y, c)
    partner = (owner(x, y, 1 - c), t)
    across = (owner(1 - x, y, c), t)
    far = (mine, z * 2 + 1 - h)
    y_peers = [(owner(x, y + i, c), t) for i in range(1, 8)]
    z_peers = [(mine, lax.rem(z + i, 8) * 2 + h) for i in range(1, 8)]
    ring = (y_peers[0], y_peers[6])
    edges = Edges(space_ref, edge_ref, relay, edge_sems)
    greet([partner, across, far] + y_peers + z_peers + edges.signalled())
    started = []

    def go(*args):
        copy = send(*args)
        started.append(copy)
        return copy

    pair = []
    for m, offset in enumerate(PAIR_ORDER):
        target = lax.rem(y + offset + 8, 8)
        pair.append(
            go(g_ref.at[:, target, 1 - c], pair_buf.at[m], pair_s.at[m], pair_r.at[m], partner)
        )
    edges.start()
    arrived = {}
    waited = set()

    def local(offset, k):
        m = PAIR_ORDER.index(offset)
        if m not in waited:
            pair[m].wait_recv()
            waited.add(m)
        return g_ref[k, lax.rem(y + offset + 8, 8), c] + pair_buf[m, k]

    for s in range(4):
        for k in range(2):
            for d in range(2):
                if s == 0 and k != d:
                    continue
                offset = 4 if s == 0 else (4 - s if d == 0 else s - 4)
                value = local(offset, k)
                if (d, k) in arrived:
                    arrived[d, k].wait_recv()
                    value = value + ring_dst[d, s - 1, k].astype(f32)
                ring_src[d, s, k] = value.astype(ring_src.dtype)
                arrived[d, k] = go(
                    ring_src.at[d, s, k],
                    ring_dst.at[d, s, k],
                    ring_s.at[d, s, k],
                    ring_r.at[d, s, k],
                    ring[d],
                )
        edges.forward(s)
        if s < 2:
            plain, weighted = pull_back(
                s, cot_ref, grad_ref, flip_ref, hat_ref, scale_ref, gain_ref, bias_ref, input_ref, back, wide
            )
            if s == 0:
                n_ref[...] = jnp.zeros_like(n_ref)
                n_ref[0:1], n_ref[1:2] = weighted, plain
            else:
                n_ref[0:1] = n_ref[0:1] + weighted
                n_ref[1:2] = n_ref[1:2] + plain
                norm_pair = go(n_ref, n_pair, one_s.at[0], one_r.at[0], partner)
        if s == 2:
            norm_pair.wait_recv()
            part = n_ref[...] + n_pair[...]
            n_y_src[...] = part
            n_y[y] = part
            norm_y = [
                go(n_y_src, n_y.at[y], ny_s.at[i], ny_r.at[i], peer)
                for i, peer in enumerate(y_peers)
            ]

    totals = []
    for k in range(2):
        value = local(0, k)
        for d in range(2):
            arrived[d, k].wait_recv()
            value = value + ring_dst[d, 3, k].astype(f32)
        totals.append(value)
    keep = jnp.where(x == 0, totals[0], totals[1])
    x_src[...] = jnp.where(x == 0, totals[1], totals[0])
    x_copy = go(x_src, x_dst, one_s.at[3], one_r.at[3], across)
    for copy in norm_y:
        copy.wait_recv()
    part = n_y[0]
    for i in range(1, 8):
        part = part + n_y[i]
    n_x_src[...] = part
    norm_x = go(n_x_src, n_x, one_s.at[1], one_r.at[1], across)
    x_copy.wait_recv()
    value = keep + x_dst[...]
    for p in range(8):
        held[p] = value[(p // 2) * 24 : (p // 2) * 24 + 24, (p % 2) * 128 : (p % 2) * 128 + 128]
    scatter = [
        go(held.at[lax.rem(z + i + 1, 8)], z_dst.at[z], zs_s.at[i], zs_r.at[i], peer)
        for i, peer in enumerate(z_peers)
    ]
    z_dst[z] = held[z]
    norm_x.wait_recv()
    part = n_x_src[...] + n_x[...]
    n_z_src[...] = part
    n_z[z] = part
    norm_z = [
        go(n_z_src, n_z.at[z], nz_s.at[i], nz_r.at[i], peer) for i, peer in enumerate(z_peers)
    ]
    for copy in scatter:
        copy.wait_recv()
    part = z_dst[0]
    for i in range(1, 8):
        part = part + z_dst[i]
    h_src[...] = part
    h_copy = go(h_src, h_dst, one_s.at[4], one_r.at[4], far)
    for copy in norm_z:
        copy.wait_recv()
    part = n_z[0]
    for i in range(1, 8):
        part = part + n_z[i]
    n_h_src[...] = part
    norm_h = go(n_h_src, n_h, one_s.at[2], one_r.at[2], far)
    h_copy.wait_recv()
    part = h_src[...] + h_dst[...]
    z_src[...] = part
    out_ref[z] = part
    spread = [
        go(z_src, out_ref.at[z], zg_s.at[i], zg_r.at[i], peer) for i, peer in enumerate(z_peers)
    ]
    norm_h.wait_recv()
    norm_ref[...] = (n_h_src[...] + n_h[...])[0:2]
    for copy in spread:
        copy.wait_recv()
    edges.finish()
    for copy in started:
        copy.wait_send()


def reduce_gradient(gradient, space, *operands):
    f32, bf16 = jnp.float32, jnp.bfloat16
    dma, vmem = pltpu.SemaphoreType.DMA, pltpu.VMEM
    small = vmem((8, 256), f32)
    eight = vmem((8, 8, 256), f32)
    return pl.pallas_call(
        reduce_kernel,
        out_shape=(
            jax.ShapeDtypeStruct((8, 24, 128), f32),
            jax.ShapeDtypeStruct((2, 256), f32),
            jax.ShapeDtypeStruct(space.shape, space.dtype),
            jax.ShapeDtypeStruct(space.shape, space.dtype),
        ),
        in_specs=[VMEM] * 9,
        out_specs=(VMEM,) * 4,
        scratch_shapes=[
            vmem((ROWS, 256), f32),
            vmem((16, PITCH, 256), bf16),
            small,
            vmem((8, 2, 96, 256), f32),
            vmem((2, 4, 2, 96, 256), bf16),
            vmem((2, 4, 2, 96, 256), bf16),
            vmem((96, 256), f32),
            vmem((96, 256), f32),
            vmem((8, 24, 128), f32),
            vmem((8, 24, 128), f32),
            vmem((24, 128), f32),
            vmem((24, 128), f32),
            vmem((24, 128), f32),
            small,
            small,
            eight,
            small,
            small,
            small,
            eight,
            small,
            small,
            dma((8,)),
            dma((8,)),
            dma((2, 4, 2)),
            dma((2, 4, 2)),
            dma((7,)),
            dma((7,)),
            dma((7,)),
            dma((7,)),
            dma((5,)),
            dma((5,)),
            dma((7,)),
            dma((7,)),
            dma((7,)),
            dma((7,)),
        ]
        + edge_scratch(space),
        compiler_params=pltpu.CompilerParams(
            collective_id=1, has_side_effects=True, vmem_limit_bytes=26 * 2**20
        ),
        name="reduce_gradient",
    )(gradient.reshape(2, 8, 2, 96, 256), space, *operands)


def block_kernel(
    clip_ref,
    cot_ref,
    edge_ref,
    w_ref,
    gain_ref,
    bias_ref,
    space_ref,
    g_ref,
    grad,
    flip,
    hat,
    scale_ref,
    cot_pad,
    wide,
    tall,
    act,
    space,
):
    f32, bf16 = jnp.float32, jnp.bfloat16
    t = lax.axis_index("tm")
    gain, bias = gain_ref[...], bias_ref[...]
    inside = (lax.broadcasted_iota(jnp.int32, (2, PITCH, 256), 1) < 36).reshape(CHUNK, 256)

    def dot(a, b, contract=(1, 0)):
        dims = (((contract[0],), (contract[1],)), ((), ()))
        return lax.dot_general(a, b, dims, preferred_element_type=f32)

    def shift(target, f):
        for j in range(3):
            for start in range(0, TALL, CHUNK):
                target[f, start : start + CHUNK, j * 256 : (j + 1) * 256] = tall[
                    start + 7 + j : start + 7 + j + CHUNK
                ].astype(bf16)

    cot_pad[...] = jnp.zeros_like(cot_pad)
    wide[...] = jnp.zeros_like(wide)
    tall[...] = jnp.zeros_like(tall)
    cot_pad[0, :, :36] = jnp.where(t == 0, 0.0, edge_ref[0].astype(f32)).astype(bf16)
    cot_pad[1, :, :36] = cot_ref[0]
    cot_pad[2, :, :36] = cot_ref[1]
    cot_pad[3, :, :36] = jnp.where(t == 15, 0.0, edge_ref[1].astype(f32)).astype(bf16)
    for i in range(3):
        for j in range(3):
            tap = 3 * i + j
            slot = 3 * i + 2 - j
            flip[slot * 256 : (slot + 1) * 256] = w_ref[tap * 256 : (tap + 1) * 256].T

    def body(start):
        return pl.ds(pl.multiple_of(start * CHUNK, CHUNK), CHUNK)

    def above(start):
        return pl.ds(pl.multiple_of(start * CHUNK + PITCH + 8, 8), CHUNK)

    def folded(value):
        return jnp.sum(value.reshape(CHUNK // 8, 8, 256), axis=0)

    def field(i):
        return wide[pl.ds(i * 2, 2)].reshape(CHUNK, 256)

    zero = jnp.zeros((8, 256), f32)
    for f in range(2):
        wide[:, :36] = clip_ref[f].astype(f32)
        total = lax.fori_loop(0, 8, lambda i, carry: carry + folded(field(i)), zero)
        center = group_mean(jnp.sum(total, axis=0, keepdims=True))

        def squares(i, carry):
            value = jnp.where(inside, field(i) - center, 0.0)
            return carry + folded(value * value)

        total = lax.fori_loop(0, 8, squares, zero)
        spread = group_mean(jnp.sum(total, axis=0, keepdims=True))
        scale = lax.rsqrt(spread + 1e-05)
        scale_ref[f : f + 1] = scale

        def activate(i, carry):
            normed = jnp.where(inside, (field(i) - center) * scale, 0.0)
            hat[f, body(i)] = normed
            u = normed * gain + bias
            value = jnp.where(inside, u / (1.0 + jnp.exp(-u)), 0.0)
            tall[above(i)] = value
            return carry

        lax.fori_loop(0, 8, activate, 0)
        shift(act, f)

    for f in range(2):
        total = dot(act[f, 0:ROWS], w_ref[0:768])
        for i in range(1, 3):
            total = total + dot(act[f, i * PITCH : i * PITCH + ROWS], w_ref[i * 768 : (i + 1) * 768])
        rounded = total.astype(bf16)
        space[f] = rounded
        space_ref[f] = rounded.reshape(16, PITCH, 256)[:, :36]

    for f in range(2):
        total = None
        for k in range(3):
            tap = w_ref[(9 + k) * 256 : (10 + k) * 256]
            term = dot(cot_pad[f + 2 - k].reshape(ROWS, 256), tap, (1, 1))
            total = term if total is None else total + term
        tall[PITCH + 8 : PITCH + 8 + ROWS] = total.astype(bf16).astype(f32)
        shift(grad, f)

    for k in range(3):
        total = None
        for f in range(2):
            term = dot(space[f], cot_pad[f + 2 - k].reshape(ROWS, 256), (0, 0))
            total = term if total is None else total + term
        g_ref[(9 + k) * 256 : (10 + k) * 256] = total
    for i in range(3):
        total = None
        for f in range(2):
            term = dot(
                act[f, i * PITCH : i * PITCH + ROWS],
                grad[f, PITCH : PITCH + ROWS, 256:512],
                (0, 0),
            )
            total = term if total is None else total + term
        g_ref[i * 768 : (i + 1) * 768] = total


def block(clips, cotangent, edges, weights, gain, bias):
    f32, bf16 = jnp.float32, jnp.bfloat16
    vmem = pltpu.VMEM
    return pl.pallas_call(
        block_kernel,
        out_shape=(
            jax.ShapeDtypeStruct(clips.shape, bf16),
            jax.ShapeDtypeStruct(weights.shape, f32),
            jax.ShapeDtypeStruct((2, TALL, 768), bf16),
            jax.ShapeDtypeStruct((2304, 256), bf16),
            jax.ShapeDtypeStruct((2, ROWS, 256), f32),
            jax.ShapeDtypeStruct((2, 256), f32),
        ),
        in_specs=[VMEM] * 6,
        out_specs=(VMEM,) * 6,
        scratch_shapes=[
            vmem((4, 16, PITCH, 256), bf16),
            vmem((16, PITCH, 256), f32),
            vmem((TALL + 16, 256), f32),
            vmem((2, TALL, 768), bf16),
            vmem((2, ROWS, 256), bf16),
        ],
        compiler_params=pltpu.CompilerParams(vmem_limit_bytes=30 * 2**20),
        name="block",
    )(clips, cotangent, edges, weights, gain, bias)


def shards(clips, cotangent, conv_master, first_moment, second_moment, norm_gain, norm_bias):
    f32 = jnp.float32
    channels = clips.shape[-1]
    clip, cot = clips[0], cotangent[0]
    rows, edges = gather_weights(conv_master.astype(jnp.bfloat16), cot)
    weights = rows.reshape(12 * channels, channels)
    gain, bias = norm_gain.reshape(1, channels), norm_bias.reshape(1, channels)
    space, local_gradient, *saved = block(clip, cot, edges, weights, gain, bias)
    pieces, norm_grads, around, input_grad = reduce_gradient(
        local_gradient, space, cot, *saved, gain, bias
    )
    gradient = pieces.reshape(4, 2, 24, 128).transpose(0, 2, 1, 3).reshape(96, channels)
    t = lax.axis_index("tm")
    zero = jnp.zeros_like(around[:1])
    padded = jnp.concatenate(
        [
            jnp.where(t == 0, zero, around[:1]),
            space,
            jnp.where(t == lax.axis_size("tm") - 1, zero, around[1:]),
        ]
    )
    temporal = clip.astype(f32)
    for frame_tap in range(3):
        tap = weights[(9 + frame_tap) * channels : (10 + frame_tap) * channels]
        temporal = temporal + jnp.einsum(
            "fhwc,cd->fhwd",
            padded[frame_tap : frame_tap + 2],
            tap,
            preferred_element_type=f32,
        )
    block_out = temporal.astype(jnp.bfloat16)[None]
    input_grad = input_grad[None]
    new_master, new_first, new_second = adam_update(
        gradient, conv_master, first_moment, second_moment
    )
    return (block_out, input_grad, new_master, new_first, new_second, norm_grads)


def solution(mesh):
    placed = (
        P("blk", "tm", None, None, None),
        P("blk", "tm", None, None, None),
        P("blk", None),
        P("blk", None),
        P("blk", None),
        P(),
        P(),
    )
    return jax.shard_map(
        shards,
        mesh=mesh,
        in_specs=placed,
        out_specs=(
            P("blk", "tm", None, None, None),
            P("blk", "tm", None, None, None),
            P("blk", None),
            P("blk", None),
            P("blk", None),
            P(),
        ),
        check_vma=False,
    )
```

```python
import jax
import jax.numpy as jnp
from jax import lax
from jax.experimental import pallas as pl
from jax.experimental.pallas import tpu as pltpu
from jax.sharding import PartitionSpec as P


beta_one = 0.9
beta_two = 0.999
learn_rate = 0.003
adam_eps = 1e-08
bias_first = 1.0 - 0.9**10
bias_second = 1.0 - 0.999**10


def adam_update(gradient, master, first, second):
    new_first = beta_one * first + (1.0 - beta_one) * gradient
    new_second = beta_two * second + (1.0 - beta_two) * gradient * gradient
    update = new_first / bias_first / (jnp.sqrt(new_second / bias_second) + adam_eps)
    return (master - learn_rate * update, new_first, new_second)

MESH = pl.DeviceIdType.MESH
VMEM = pl.BlockSpec(memory_space=pltpu.VMEM)


def place():
    me = lax.axis_index("blk")
    return me // 16, lax.rem(me // 2, 8), lax.rem(me, 2), lax.axis_index("tm")


def owner(x, y, c):
    return x * 16 + lax.rem(y + 8, 8) * 2 + c


def greet(peers):
    barrier = pltpu.get_barrier_semaphore()
    for peer in peers:
        pl.semaphore_signal(barrier, inc=1, device_id=peer, device_id_type=MESH)
    pl.semaphore_wait(barrier, len(peers))


def send(src, dst, send_sem, recv_sem, peer):
    copy = pltpu.make_async_remote_copy(
        src_ref=src,
        dst_ref=dst,
        send_sem=send_sem,
        recv_sem=recv_sem,
        device_id=peer,
        device_id_type=MESH,
    )
    copy.start()
    return copy


def at_chip(position, y, c, t):
    position = lax.rem(position + 4, 4)
    t = lax.rem(t + 16, 16)
    return owner(lax.rem(position, 2), y, c), (t // 2) * 2 + position // 2


class Edges:
    def __init__(self, frames, edges, relay, sems):
        self.frames, self.edges, self.relay, self.sems = frames, edges, relay, sems
        x, y, c, t = place()
        here = lax.rem(t, 2) * 2 + x
        self.near, self.last, self.source = [], [], []
        for step in (1, -1):
            z = t // 2
            origin = lax.rem(here - step + 4, 4)
            t_origin = z * 2 + origin // 2
            t_last = lax.rem(t_origin + step + 16, 16)
            self.near.append(at_chip(here + step, y, c, t))
            self.last.append((owner(lax.rem(origin, 2), y, c), t_last))
            self.source.append(at_chip(here - step, y, c, t - step))

    def signalled(self):
        return self.near + self.source

    def start(self):
        first_s, first_r, _, _ = self.sems
        self.first, self.second = {}, []
        for q in range(4):
            for d in range(2):
                rows = pl.ds(q * 4, 4)
                self.first[d, q] = send(
                    self.frames.at[1 - d, rows],
                    self.relay.at[d, rows],
                    first_s.at[d, q],
                    first_r.at[d, q],
                    self.near[d],
                )

    def forward(self, q):
        _, _, second_s, second_r = self.sems
        for d in range(2):
            rows = pl.ds(q * 4, 4)
            self.first[d, q].wait_recv()
            self.second.append(
                send(
                    self.relay.at[d, rows],
                    self.edges.at[d, rows],
                    second_s.at[d, q],
                    second_r.at[d, q],
                    self.last[d],
                )
            )

    def finish(self):
        for copy in self.second:
            copy.wait()
        for copy in self.first.values():
            copy.wait_send()


def edge_scratch(frames):
    dma = pltpu.SemaphoreType.DMA
    return [pltpu.VMEM(frames.shape, frames.dtype)] + [dma((2, 4))] * 4


PITCH = 48
ROWS = 16 * PITCH
TALL = ROWS + 2 * PITCH
CHUNK = 2 * PITCH


def group_mean(row):
    rows = lax.broadcasted_iota(jnp.int32, (256, 256), 0) // 8
    columns = lax.broadcasted_iota(jnp.int32, (256, 256), 1) // 8
    same = (rows == columns).astype(jnp.float32)
    total = jnp.dot(
        jnp.broadcast_to(row, (8, 256)),
        same,
        precision=lax.Precision.HIGHEST,
        preferred_element_type=jnp.float32,
    )
    return total[0:1] * (1.0 / (16 * 36 * 8))


def shift(tall, target, f):
    for j in range(3):
        for start in range(0, TALL, CHUNK):
            target[f, start : start + CHUNK, j * 256 : (j + 1) * 256] = tall[
                start + 7 + j : start + 7 + j + CHUNK
            ].astype(jnp.bfloat16)


def norm_forward(f, clip_ref, gain_ref, bias_ref, act, hat, scale_ref, wide, tall):
    f32 = jnp.float32
    gain, bias = gain_ref[...], bias_ref[...]
    inside = (lax.broadcasted_iota(jnp.int32, (2, PITCH, 256), 1) < 36).reshape(CHUNK, 256)
    zero = jnp.zeros((8, 256), f32)
    wide[...] = jnp.zeros_like(wide)
    tall[...] = jnp.zeros_like(tall)
    wide[:, :36] = clip_ref[f].astype(f32)

    def body(start):
        return pl.ds(pl.multiple_of(start * CHUNK, CHUNK), CHUNK)

    def above(start):
        return pl.ds(pl.multiple_of(start * CHUNK + PITCH + 8, 8), CHUNK)

    def folded(value):
        return jnp.sum(value.reshape(CHUNK // 8, 8, 256), axis=0)

    def field(i):
        return wide[pl.ds(i * 2, 2)].reshape(CHUNK, 256)

    total = lax.fori_loop(0, 8, lambda i, carry: carry + folded(field(i)), zero)
    center = group_mean(jnp.sum(total, axis=0, keepdims=True))

    def squares(i, carry):
        value = jnp.where(inside, field(i) - center, 0.0)
        return carry + folded(value * value)

    total = lax.fori_loop(0, 8, squares, zero)
    spread = group_mean(jnp.sum(total, axis=0, keepdims=True))
    scale = lax.rsqrt(spread + 1e-05)
    scale_ref[f : f + 1] = scale

    def activate(i, carry):
        normed = jnp.where(inside, (field(i) - center) * scale, 0.0)
        hat[f, body(i)] = normed
        u = normed * gain + bias
        value = jnp.where(inside, u / (1.0 + jnp.exp(-u)), 0.0)
        tall[above(i)] = value
        return carry

    lax.fori_loop(0, 8, activate, 0)
    shift(tall, act, f)


def gather_kernel(
    w_ref,
    cot_ref,
    clip_ref,
    gain_ref,
    bias_ref,
    out_ref,
    edge_ref,
    act_ref,
    hat_ref,
    scale_ref,
    wide,
    tall,
    ring_send,
    ring_recv,
    pair_send,
    pair_recv,
    x_send,
    x_recv,
    relay,
    *edge_sems,
):
    x, y, c, t = place()
    partner = (owner(x, y, 1 - c), t)
    across = (owner(1 - x, y, c), t)
    ring = ((owner(x, y + 1, c), t), (owner(x, y - 1, c), t))
    edges = Edges(cot_ref, edge_ref, relay, edge_sems)
    greet([partner, across, ring[0], ring[1]] + edges.signalled())
    started = []

    def pass_on(src, k, offset):
        slot = k * 8 + offset % 8
        dst = out_ref.at[owner(x if k == 0 else 1 - x, y + offset, c)]
        started.append(send(src, dst, pair_send.at[slot], pair_recv.at[slot], partner))

    def hop(src, d, s, k):
        offset = -s if d == 0 else s
        dst = out_ref.at[owner(x if k == 0 else 1 - x, y + offset, c)]
        copy = send(src, dst, ring_send.at[d, s, k], ring_recv.at[d, s, k], ring[d])
        started.append(copy)
        return copy

    mine = owner(x, y, c)
    x_copy = send(w_ref, out_ref.at[mine], x_send, x_recv, across)
    copies = {}
    for d in range(2):
        copies[d, 0] = hop(w_ref, d, 0, 0)
    pass_on(w_ref, 0, 0)
    edges.start()
    saved = clip_ref, gain_ref, bias_ref, act_ref, hat_ref, scale_ref, wide, tall
    norm_forward(0, *saved)
    out_ref[mine] = w_ref[...]
    x_copy.wait_recv()
    other = out_ref.at[owner(1 - x, y, c)]
    for d in range(2):
        copies[d, 1] = hop(other, d, 0, 1)
    pass_on(other, 1, 0)
    for s in range(1, 5):
        for k in range(2):
            for d in range(2):
                if s == 4 and k != d:
                    continue
                offset = -s if d == 0 else s
                copies[d, k].wait_recv()
                block = out_ref.at[owner(x if k == 0 else 1 - x, y + offset, c)]
                if s < 3 or (s == 3 and k == d):
                    copies[d, k] = hop(block, d, s, k)
                pass_on(block, k, offset)
        edges.forward(s - 1)
        if s == 1:
            norm_forward(1, *saved)
    x_copy.wait_send()
    for copy in started:
        copy.wait_send()
    for slot in range(16):
        k, offset = slot // 8, slot % 8
        block = out_ref.at[owner(x if k == 0 else 1 - x, y + offset, 1 - c)]
        pltpu.make_async_remote_copy(
            src_ref=w_ref,
            dst_ref=block,
            send_sem=pair_send.at[slot],
            recv_sem=pair_recv.at[slot],
            device_id=partner,
            device_id_type=MESH,
        ).wait_recv()
    edges.finish()


def gather_weights(rows, cotangent, clips, gain, bias):
    dma = pltpu.SemaphoreType.DMA
    return pl.pallas_call(
        gather_kernel,
        out_shape=(
            jax.ShapeDtypeStruct((32,) + rows.shape, rows.dtype),
            jax.ShapeDtypeStruct(cotangent.shape, cotangent.dtype),
            jax.ShapeDtypeStruct((2, TALL, 768), jnp.bfloat16),
            jax.ShapeDtypeStruct((2, ROWS, 256), jnp.float32),
            jax.ShapeDtypeStruct((2, 256), jnp.float32),
        ),
        in_specs=[VMEM] * 5,
        out_specs=(VMEM,) * 5,
        scratch_shapes=[
            pltpu.VMEM((16, PITCH, 256), jnp.float32),
            pltpu.VMEM((TALL + 16, 256), jnp.float32),
            dma((2, 4, 2)),
            dma((2, 4, 2)),
            dma((16,)),
            dma((16,)),
            dma(()),
            dma(()),
        ]
        + edge_scratch(cotangent),
        compiler_params=pltpu.CompilerParams(
            collective_id=0, has_side_effects=True, vmem_limit_bytes=18 * 2**20
        ),
        name="gather_weights",
    )(rows, cotangent, clips, gain, bias)


def pull_back(
    f, cot_ref, grad_ref, flip_ref, hat_ref, scale_ref, gain_ref, bias_ref, input_ref, back, wide
):
    f32, bf16 = jnp.float32, jnp.bfloat16
    gain, bias = gain_ref[...], bias_ref[...]
    inside = (lax.broadcasted_iota(jnp.int32, (2, PITCH, 256), 1) < 36).reshape(CHUNK, 256)
    zero = jnp.zeros((8, 256), f32)
    total = None
    for i in range(3):
        low = (2 - i) * PITCH
        term = jnp.dot(
            grad_ref[f, low : low + ROWS],
            flip_ref[i * 768 : (i + 1) * 768],
            preferred_element_type=f32,
        )
        total = term if total is None else total + term
    back[...] = total
    wide[...] = jnp.zeros_like(wide)
    wide[:, :36] = cot_ref[f]

    def body(start):
        return pl.ds(pl.multiple_of(start * CHUNK, CHUNK), CHUNK)

    def folded(value):
        return jnp.sum(value.reshape(CHUNK // 8, 8, 256), axis=0)

    def pull(i, carry):
        normed = hat_ref[f, body(i)]
        u = normed * gain + bias
        gate = 1.0 / (1.0 + jnp.exp(-u))
        down = jnp.where(inside, back[body(i)] * (gate * (1.0 + u * (1.0 - gate))), 0.0)
        back[body(i)] = down
        return carry[0] + folded(down), carry[1] + folded(down * normed)

    plain, weighted = lax.fori_loop(0, 8, pull, (zero, zero))
    plain = jnp.sum(plain, axis=0, keepdims=True)
    weighted = jnp.sum(weighted, axis=0, keepdims=True)
    plain_mean, weighted_mean = group_mean(gain * plain), group_mean(gain * weighted)
    scale = scale_ref[f : f + 1]

    def finish(i, carry):
        term = scale * (back[body(i)] * gain - plain_mean - hat_ref[f, body(i)] * weighted_mean)
        pair = wide[pl.ds(i * 2, 2)].reshape(CHUNK, 256)
        result = (pair.astype(f32) + term).reshape(2, PITCH, 256)[:, :36]
        input_ref[f, pl.ds(i * 2, 2)] = result.astype(bf16)
        return carry

    lax.fori_loop(0, 8, finish, 0)
    return plain, weighted


PAIR_ORDER = (4, 3, -3, 2, -2, 1, -1, 0)


def reduce_kernel(
    g_ref,
    space_ref,
    cot_ref,
    grad_ref,
    flip_ref,
    hat_ref,
    scale_ref,
    gain_ref,
    bias_ref,
    out_ref,
    norm_ref,
    edge_ref,
    input_ref,
    back,
    wide,
    n_ref,
    pair_buf,
    ring_src,
    ring_dst,
    x_src,
    x_dst,
    held,
    z_dst,
    h_src,
    h_dst,
    z_src,
    n_pair,
    n_y_src,
    n_y,
    n_x_src,
    n_x,
    n_z_src,
    n_z,
    n_h_src,
    n_h,
    pair_s,
    pair_r,
    ring_s,
    ring_r,
    zs_s,
    zs_r,
    zg_s,
    zg_r,
    one_s,
    one_r,
    ny_s,
    ny_r,
    nz_s,
    nz_r,
    relay,
    *edge_sems,
):
    f32 = jnp.float32
    x, y, c, t = place()
    z, h = t // 2, lax.rem(t, 2)
    mine = owner(x, y, c)
    partner = (owner(x, y, 1 - c), t)
    across = (owner(1 - x, y, c), t)
    far = (mine, z * 2 + 1 - h)
    y_peers = [(owner(x, y + i, c), t) for i in range(1, 8)]
    z_peers = [(mine, lax.rem(z + i, 8) * 2 + h) for i in range(1, 8)]
    ring = (y_peers[0], y_peers[6])
    edges = Edges(space_ref, edge_ref, relay, edge_sems)
    greet([partner, across, far] + y_peers + z_peers + edges.signalled())
    started = []

    def go(*args):
        copy = send(*args)
        started.append(copy)
        return copy

    pair = []
    for m, offset in enumerate(PAIR_ORDER):
        target = lax.rem(y + offset + 8, 8)
        pair.append(
            go(g_ref.at[:, target, 1 - c], pair_buf.at[m], pair_s.at[m], pair_r.at[m], partner)
        )
    edges.start()
    arrived = {}
    waited = set()

    def local(offset, k):
        m = PAIR_ORDER.index(offset)
        if m not in waited:
            pair[m].wait_recv()
            waited.add(m)
        return g_ref[k, lax.rem(y + offset + 8, 8), c] + pair_buf[m, k]

    for s in range(4):
        for k in range(2):
            for d in range(2):
                if s == 0 and k != d:
                    continue
                offset = 4 if s == 0 else (4 - s if d == 0 else s - 4)
                value = local(offset, k)
                if (d, k) in arrived:
                    arrived[d, k].wait_recv()
                    value = value + ring_dst[d, s - 1, k].astype(f32)
                ring_src[d, s, k] = value.astype(ring_src.dtype)
                arrived[d, k] = go(
                    ring_src.at[d, s, k],
                    ring_dst.at[d, s, k],
                    ring_s.at[d, s, k],
                    ring_r.at[d, s, k],
                    ring[d],
                )
        edges.forward(s)
        if s < 2:
            plain, weighted = pull_back(
                s, cot_ref, grad_ref, flip_ref, hat_ref, scale_ref, gain_ref, bias_ref, input_ref, back, wide
            )
            if s == 0:
                n_ref[...] = jnp.zeros_like(n_ref)
                n_ref[0:1], n_ref[1:2] = weighted, plain
            else:
                n_ref[0:1] = n_ref[0:1] + weighted
                n_ref[1:2] = n_ref[1:2] + plain
                norm_pair = go(n_ref, n_pair, one_s.at[0], one_r.at[0], partner)
        if s == 2:
            norm_pair.wait_recv()
            part = n_ref[...] + n_pair[...]
            n_y_src[...] = part
            n_y[y] = part
            norm_y = [
                go(n_y_src, n_y.at[y], ny_s.at[i], ny_r.at[i], peer)
                for i, peer in enumerate(y_peers)
            ]

    totals = []
    for k in range(2):
        value = local(0, k)
        for d in range(2):
            arrived[d, k].wait_recv()
            value = value + ring_dst[d, 3, k].astype(f32)
        totals.append(value)
    keep = jnp.where(x == 0, totals[0], totals[1])
    x_src[...] = jnp.where(x == 0, totals[1], totals[0])
    x_copy = go(x_src, x_dst, one_s.at[3], one_r.at[3], across)
    for copy in norm_y:
        copy.wait_recv()
    part = n_y[0]
    for i in range(1, 8):
        part = part + n_y[i]
    n_x_src[...] = part
    norm_x = go(n_x_src, n_x, one_s.at[1], one_r.at[1], across)
    x_copy.wait_recv()
    value = keep + x_dst[...]
    for p in range(8):
        held[p] = value[(p // 2) * 24 : (p // 2) * 24 + 24, (p % 2) * 128 : (p % 2) * 128 + 128]
    scatter = [
        go(held.at[lax.rem(z + i + 1, 8)], z_dst.at[z], zs_s.at[i], zs_r.at[i], peer)
        for i, peer in enumerate(z_peers)
    ]
    z_dst[z] = held[z]
    norm_x.wait_recv()
    part = n_x_src[...] + n_x[...]
    n_z_src[...] = part
    n_z[z] = part
    norm_z = [
        go(n_z_src, n_z.at[z], nz_s.at[i], nz_r.at[i], peer) for i, peer in enumerate(z_peers)
    ]
    for copy in scatter:
        copy.wait_recv()
    part = z_dst[0]
    for i in range(1, 8):
        part = part + z_dst[i]
    h_src[...] = part
    h_copy = go(h_src, h_dst, one_s.at[4], one_r.at[4], far)
    for copy in norm_z:
        copy.wait_recv()
    part = n_z[0]
    for i in range(1, 8):
        part = part + n_z[i]
    n_h_src[...] = part
    norm_h = go(n_h_src, n_h, one_s.at[2], one_r.at[2], far)
    h_copy.wait_recv()
    part = h_src[...] + h_dst[...]
    z_src[...] = part
    out_ref[z] = part
    spread = [
        go(z_src, out_ref.at[z], zg_s.at[i], zg_r.at[i], peer) for i, peer in enumerate(z_peers)
    ]
    norm_h.wait_recv()
    norm_ref[...] = (n_h_src[...] + n_h[...])[0:2]
    for copy in spread:
        copy.wait_recv()
    edges.finish()
    for copy in started:
        copy.wait_send()


def reduce_gradient(gradient, space, *operands):
    f32, bf16 = jnp.float32, jnp.bfloat16
    dma, vmem = pltpu.SemaphoreType.DMA, pltpu.VMEM
    small = vmem((8, 256), f32)
    eight = vmem((8, 8, 256), f32)
    return pl.pallas_call(
        reduce_kernel,
        out_shape=(
            jax.ShapeDtypeStruct((8, 24, 128), f32),
            jax.ShapeDtypeStruct((2, 256), f32),
            jax.ShapeDtypeStruct(space.shape, space.dtype),
            jax.ShapeDtypeStruct(space.shape, space.dtype),
        ),
        in_specs=[VMEM] * 9,
        out_specs=(VMEM,) * 4,
        scratch_shapes=[
            vmem((ROWS, 256), f32),
            vmem((16, PITCH, 256), bf16),
            small,
            vmem((8, 2, 96, 256), f32),
            vmem((2, 4, 2, 96, 256), bf16),
            vmem((2, 4, 2, 96, 256), bf16),
            vmem((96, 256), f32),
            vmem((96, 256), f32),
            vmem((8, 24, 128), f32),
            vmem((8, 24, 128), f32),
            vmem((24, 128), f32),
            vmem((24, 128), f32),
            vmem((24, 128), f32),
            small,
            small,
            eight,
            small,
            small,
            small,
            eight,
            small,
            small,
            dma((8,)),
            dma((8,)),
            dma((2, 4, 2)),
            dma((2, 4, 2)),
            dma((7,)),
            dma((7,)),
            dma((7,)),
            dma((7,)),
            dma((5,)),
            dma((5,)),
            dma((7,)),
            dma((7,)),
            dma((7,)),
            dma((7,)),
        ]
        + edge_scratch(space),
        compiler_params=pltpu.CompilerParams(
            collective_id=1, has_side_effects=True, vmem_limit_bytes=26 * 2**20
        ),
        name="reduce_gradient",
    )(gradient.reshape(2, 8, 2, 96, 256), space, *operands)


def block_kernel(
    act,
    cot_ref,
    edge_ref,
    w_ref,
    space_ref,
    g_ref,
    grad,
    flip,
    cot_pad,
    tall,
    space,
):
    f32, bf16 = jnp.float32, jnp.bfloat16
    t = lax.axis_index("tm")
    def dot(a, b, contract=(1, 0)):
        dims = (((contract[0],), (contract[1],)), ((), ()))
        return lax.dot_general(a, b, dims, preferred_element_type=f32)

    cot_pad[...] = jnp.zeros_like(cot_pad)
    tall[...] = jnp.zeros_like(tall)
    cot_pad[0, :, :36] = jnp.where(t == 0, 0.0, edge_ref[0].astype(f32)).astype(bf16)
    cot_pad[1, :, :36] = cot_ref[0]
    cot_pad[2, :, :36] = cot_ref[1]
    cot_pad[3, :, :36] = jnp.where(t == 15, 0.0, edge_ref[1].astype(f32)).astype(bf16)
    for i in range(3):
        for j in range(3):
            tap = 3 * i + j
            slot = 3 * i + 2 - j
            flip[slot * 256 : (slot + 1) * 256] = w_ref[tap * 256 : (tap + 1) * 256].T

    for f in range(2):
        total = dot(act[f, 0:ROWS], w_ref[0:768])
        for i in range(1, 3):
            total = total + dot(act[f, i * PITCH : i * PITCH + ROWS], w_ref[i * 768 : (i + 1) * 768])
        rounded = total.astype(bf16)
        space[f] = rounded
        space_ref[f] = rounded.reshape(16, PITCH, 256)[:, :36]

    for f in range(2):
        total = None
        for k in range(3):
            tap = w_ref[(9 + k) * 256 : (10 + k) * 256]
            term = dot(cot_pad[f + 2 - k].reshape(ROWS, 256), tap, (1, 1))
            total = term if total is None else total + term
        tall[PITCH + 8 : PITCH + 8 + ROWS] = total.astype(bf16).astype(f32)
        shift(tall, grad, f)

    for k in range(3):
        total = None
        for f in range(2):
            term = dot(space[f], cot_pad[f + 2 - k].reshape(ROWS, 256), (0, 0))
            total = term if total is None else total + term
        g_ref[(9 + k) * 256 : (10 + k) * 256] = total
    for i in range(3):
        total = None
        for f in range(2):
            term = dot(
                act[f, i * PITCH : i * PITCH + ROWS],
                grad[f, PITCH : PITCH + ROWS, 256:512],
                (0, 0),
            )
            total = term if total is None else total + term
        g_ref[i * 768 : (i + 1) * 768] = total


def block(act, cotangent, edges, weights):
    f32, bf16 = jnp.float32, jnp.bfloat16
    vmem = pltpu.VMEM
    return pl.pallas_call(
        block_kernel,
        out_shape=(
            jax.ShapeDtypeStruct(cotangent.shape, bf16),
            jax.ShapeDtypeStruct(weights.shape, f32),
            jax.ShapeDtypeStruct((2, TALL, 768), bf16),
            jax.ShapeDtypeStruct((2304, 256), bf16),
        ),
        in_specs=[VMEM] * 4,
        out_specs=(VMEM,) * 4,
        scratch_shapes=[
            vmem((4, 16, PITCH, 256), bf16),
            vmem((TALL + 16, 256), f32),
            vmem((2, ROWS, 256), bf16),
        ],
        compiler_params=pltpu.CompilerParams(vmem_limit_bytes=30 * 2**20),
        name="block",
    )(act, cotangent, edges, weights)


def shards(clips, cotangent, conv_master, first_moment, second_moment, norm_gain, norm_bias):
    f32 = jnp.float32
    channels = clips.shape[-1]
    clip, cot = clips[0], cotangent[0]
    gain, bias = norm_gain.reshape(1, channels), norm_bias.reshape(1, channels)
    rows, edges, act, hat, scale = gather_weights(
        conv_master.astype(jnp.bfloat16), cot, clip, gain, bias
    )
    weights = rows.reshape(12 * channels, channels)
    space, local_gradient, grad, flip = block(act, cot, edges, weights)
    pieces, norm_grads, around, input_grad = reduce_gradient(
        local_gradient, space, cot, grad, flip, hat, scale, gain, bias
    )
    gradient = pieces.reshape(4, 2, 24, 128).transpose(0, 2, 1, 3).reshape(96, channels)
    t = lax.axis_index("tm")
    zero = jnp.zeros_like(around[:1])
    padded = jnp.concatenate(
        [
            jnp.where(t == 0, zero, around[:1]),
            space,
            jnp.where(t == lax.axis_size("tm") - 1, zero, around[1:]),
        ]
    )
    temporal = clip.astype(f32)
    for frame_tap in range(3):
        tap = weights[(9 + frame_tap) * channels : (10 + frame_tap) * channels]
        temporal = temporal + jnp.einsum(
            "fhwc,cd->fhwd",
            padded[frame_tap : frame_tap + 2],
            tap,
            preferred_element_type=f32,
        )
    block_out = temporal.astype(jnp.bfloat16)[None]
    input_grad = input_grad[None]
    new_master, new_first, new_second = adam_update(
        gradient, conv_master, first_moment, second_moment
    )
    return (block_out, input_grad, new_master, new_first, new_second, norm_grads)


def solution(mesh):
    placed = (
        P("blk", "tm", None, None, None),
        P("blk", "tm", None, None, None),
        P("blk", None),
        P("blk", None),
        P("blk", None),
        P(),
        P(),
    )
    return jax.shard_map(
        shards,
        mesh=mesh,
        in_specs=placed,
        out_specs=(
            P("blk", "tm", None, None, None),
            P("blk", "tm", None, None, None),
            P("blk", None),
            P("blk", None),
            P("blk", None),
            P(),
        ),
        check_vma=False,
    )
```
